32 devices in a mesh: gx: 4 (over x, core), gy: 4 (over z), gz: 2 (over y).
Axes of the slice: x: 2, y: 2, z: 4, core: 2. Of those that a mesh axis runs over, the one named last changes fastest.
Arguments:
- prior_basis: float32 [16, 64, 3072], P('gx', 'gy', 'gz'), may hold values from -6 to 6
- edge_weights: float32 [3, 16, 64, 32], P(None, 'gx', 'gy', 'gz'), may hold values from 0.5 to 1.5
- spectral_shift: float32 [1], replicated, may hold values from 0.5 to 4
Outputs:
- new_basis: float32 [16, 64, 4096], P('gx', 'gy', 'gz')
- projection: float32 [96, 128], replicated
- triangle: float32 [128, 128], replicated
The draws below stay inside these ranges and needn't reach their ends.
All inputs are finite; a program needn't handle non-finite values.
Results may differ from the reference program's by a relative error of at most 0.002.
Values sent between devices are 32-bit elements; how exact they have to be, the bound alone decides.
No kernel may reach another device: no remote copies, remote signals or barrier semaphores. Data moves between devices by JAX's collectives and lax.ppermute only.
A program may use at most 64 MiB of HBM per device.

```python
import math
import jax
import jax.numpy as jnp
from jax import lax

BLOCK = 32
POWERS = 4
PRIOR = 3
BASIS = 96
NX = 16
NY = 64
NZ = 32


def draw_prior_basis(key, part):
    key_own = jax.random.fold_in(key, 11)
    key_shared = jax.random.fold_in(key, 12)
    own_part = jnp.clip(jax.random.normal(key_own, (NX, NY, NZ, PRIOR, BLOCK), jnp.float32), -4.0, 4.0)
    shared_part = jnp.clip(jax.random.normal(key_shared, (NX, NY, NZ, 1, BLOCK), jnp.float32), -4.0, 4.0)
    mixed = own_part + 0.15 * shared_part
    return mixed.reshape(NX, NY, NZ * PRIOR * BLOCK)


def steps_of(own_key, shape, cuts, low, high):
    gain, own = 1.0, jax.random.fold_in(own_key, 6)
    for axis_at, blocks in cuts:
        draws = jnp.exp(jax.random.uniform(jax.random.fold_in(own, axis_at), (blocks,), jnp.float32, low / len(cuts), high / len(cuts)))
        gain = gain * jnp.repeat(draws, shape[axis_at] // blocks).reshape([-1 if axis == axis_at else 1 for axis in range(len(shape))])
    return gain


def setup_inputs(seed: int = 0) -> dict:
    arg_keys = jax.random.split(jax.random.key(seed), 4)
    prior_basis = draw_prior_basis(jax.random.fold_in(arg_keys[3], 71), 0)
    edge_weights = jnp.clip(jnp.exp(math.log(1.5) - 1.0986123 * jax.random.uniform(arg_keys[1], (3, NX, NY, NZ), jnp.float32) ** steps_of(arg_keys[1], (3, NX, NY, NZ), ((1, 4), (2, 4), (3, 2)), -0.2, 0.2)), 0.5, 1.5)
    spectral_shift = jnp.clip(jnp.exp(jax.random.uniform(arg_keys[2], (1,), jnp.float32, math.log(0.5), math.log(4.0))), 0.5, 4.0)
    return {"prior_basis": prior_basis, "edge_weights": edge_weights, "spectral_shift": spectral_shift}


PRECISE = lax.Precision.HIGHEST
OPERATOR_SCALE = 11.0

def apply_operator(field, weight_pad, shift_value):
    padded = jnp.pad(field, ((1, 1), (1, 1), (1, 1), (0, 0)))
    centre = field
    summed = weight_pad[0, 1:-1, 1:-1, 1:-1] * (centre - padded[2:, 1:-1, 1:-1]) + weight_pad[0, :-2, 1:-1, 1:-1] * (centre - padded[:-2, 1:-1, 1:-1])
    summed = summed + weight_pad[1, 1:-1, 1:-1, 1:-1] * (centre - padded[1:-1, 2:, 1:-1]) + weight_pad[1, 1:-1, :-2, 1:-1] * (centre - padded[1:-1, :-2, 1:-1])
    summed = summed + weight_pad[2, 1:-1, 1:-1, 1:-1] * (centre - padded[1:-1, 1:-1, 2:]) + weight_pad[2, 1:-1, 1:-1, :-2] * (centre - padded[1:-1, 1:-1, :-2])
    return (summed + shift_value * centre) / OPERATOR_SCALE - centre

def reference(prior_basis, edge_weights, spectral_shift):
    cell_count = NX * NY * NZ
    basis_rows = prior_basis.reshape(cell_count, BASIS)
    start_block = prior_basis.reshape(NX, NY, NZ, BASIS)[..., BASIS - BLOCK:]
    weight_pad = jnp.pad(edge_weights, ((0, 0), (1, 1), (1, 1), (1, 1)))[..., None]
    shift_value = spectral_shift[0]
    previous = start_block
    current = apply_operator(start_block, weight_pad, shift_value)
    powers = [current]
    for degree in range(1, POWERS):
        following = 2.0 * apply_operator(current, weight_pad, shift_value) - previous
        previous, current = (current, following)
        powers.append(following)
    krylov = jnp.stack(powers, axis=3).reshape(cell_count, BLOCK * POWERS)
    first_coef = jnp.dot(basis_rows.T, krylov, precision=PRECISE) / cell_count
    once = krylov - jnp.dot(basis_rows, first_coef, precision=PRECISE)
    second_coef = jnp.dot(basis_rows.T, once, precision=PRECISE) / cell_count
    twice = once - jnp.dot(basis_rows, second_coef, precision=PRECISE)
    gram_matrix = jnp.dot(twice.T, twice, precision=PRECISE) / cell_count
    lower_factor = jnp.linalg.cholesky(gram_matrix)
    solved = jax.scipy.linalg.solve_triangular(lower_factor, twice.T, lower=True)
    new_basis = solved.T.reshape(NX, NY, NZ * BLOCK * POWERS)
    return (new_basis, first_coef + second_coef, lower_factor.T)
```

```python
import jax
import jax.numpy as jnp
from jax import lax
from jax.sharding import PartitionSpec as P

BLOCK = 32
POWERS = 4
BASIS = 96


PRECISE = lax.Precision.HIGHEST
OPERATOR_SCALE = 11.0


DEGREE = 6.0


def precise(left, right):
    return jnp.dot(left, right, precision=PRECISE)


def basis_change(centre, width):
    zero = jnp.zeros_like(centre)
    one = zero + 1.0

    def apply_a(c):
        up = [zero] + [width * v for v in c[:-1]]
        down = [width * v for v in c[1:]] + [zero]
        return [centre * v + u + d for v, u, d in zip(c, up, down)]

    def apply_x(c):
        out = [zero] * len(c)
        out[1] = out[1] + c[0]
        for k in range(1, len(c)):
            if k + 1 < len(c):
                out[k + 1] = out[k + 1] + 0.5 * c[k]
            out[k - 1] = out[k - 1] + 0.5 * c[k]
        return [(o - centre * v) * (1.0 / width) for o, v in zip(out, c)]

    t = [[one] + [zero] * POWERS]
    t.append(apply_a(t[0]))
    s = [[one] + [zero] * POWERS]
    s.append(apply_x(s[0]))
    for _ in range(1, POWERS):
        t.append([2.0 * v - w for v, w in zip(apply_a(t[-1]), t[-2])])
        s.append([v - w for v, w in zip(apply_x(s[-1]), s[-2])])
    to_power = jnp.stack([jnp.stack([t[k][j] for k in range(1, POWERS + 1)]) for j in range(1, POWERS + 1)])
    constant = jnp.stack([t[k][0] for k in range(1, POWERS + 1)])[None]
    removed = -jnp.stack([s[j][0] for j in range(1, POWERS + 1)])[None]
    return to_power, constant, removed


def total(values):
    for axis in ("gx", "gz", "gy"):
        count = lax.axis_size(axis)
        if count & (count - 1):
            values = lax.psum(values, axis)
            continue
        step = 1
        while step < count:
            values = values + lax.ppermute(values, axis, [(i, i ^ step) for i in range(count)])
            step *= 2
    return values


def with_halo(block, sides, width):
    for axis, dim in sides:
        count = lax.axis_size(axis)
        forward = [(i, i + 1) for i in range(count - 1)]
        backward = [(target, source) for source, target in forward]
        low = lax.ppermute(
            lax.slice_in_dim(block, block.shape[dim] - width, None, axis=dim), axis, forward
        )
        high = lax.ppermute(lax.slice_in_dim(block, 0, width, axis=dim), axis, backward)
        block = jnp.concatenate([low, block, high], axis=dim)
    return block


def crop_margin(values, layers, columns):
    if layers == 0:
        return values
    return values[
        ...,
        layers : values.shape[-3] - layers,
        layers : values.shape[-2] - layers,
        layers * columns : values.shape[-1] - layers * columns,
    ]


def stencil(padded, weight_pad, shift_value, columns):
    centre = crop_margin(padded, 1, columns)
    inner_weights = crop_margin(weight_pad, 1, columns)
    below_x = weight_pad[0, :-2, 1:-1, columns:-columns]
    below_y = weight_pad[1, 1:-1, :-2, columns:-columns]
    below_z = weight_pad[2, 1:-1, 1:-1, : -2 * columns]
    summed = inner_weights[0] * (centre - padded[2:, 1:-1, columns:-columns]) + below_x * (
        centre - padded[:-2, 1:-1, columns:-columns]
    )
    summed = (
        summed
        + inner_weights[1] * (centre - padded[1:-1, 2:, columns:-columns])
        + below_y * (centre - padded[1:-1, :-2, columns:-columns])
    )
    summed = (
        summed
        + inner_weights[2] * (centre - padded[1:-1, 1:-1, 2 * columns :])
        + below_z * (centre - padded[1:-1, 1:-1, : -2 * columns])
    )
    return (summed + shift_value * centre) / OPERATOR_SCALE - centre


def line_inside(local_count, margin, position, device_count):
    positions = (
        jnp.arange(local_count + 2 * margin, dtype=jnp.int32) + position * local_count - margin
    )
    return ((positions >= 0) & (positions < local_count * device_count)).astype(jnp.float32)


def per_device(prior_basis, edge_weights, spectral_shift):
    size_x = prior_basis.shape[0]
    size_y = prior_basis.shape[1]
    size_z = prior_basis.shape[2] // BASIS
    cell_local = size_x * size_y * size_z
    cell_count = cell_local * lax.axis_size("gx") * lax.axis_size("gy") * lax.axis_size("gz")
    shift_value = spectral_shift[0]
    basis_rows = prior_basis.reshape(cell_local, BASIS)
    start_block = prior_basis.reshape(size_x, size_y, size_z, BASIS)[..., BASIS - BLOCK :]
    weight_pad = with_halo(edge_weights, (("gx", 1), ("gy", 2), ("gz", 3)), POWERS)
    weight_pad = jnp.repeat(weight_pad, BLOCK, axis=3)
    padded = with_halo(start_block, (("gx", 0), ("gy", 1), ("gz", 2)), POWERS)
    padded = padded.reshape(size_x + 2 * POWERS, size_y + 2 * POWERS, (size_z + 2 * POWERS) * BLOCK)
    inside_x = line_inside(size_x, POWERS, lax.axis_index("gx"), lax.axis_size("gx"))
    inside_y = line_inside(size_y, POWERS, lax.axis_index("gy"), lax.axis_size("gy"))
    inside_z = jnp.repeat(
        line_inside(size_z, POWERS, lax.axis_index("gz"), lax.axis_size("gz")), BLOCK
    )
    inside = inside_x[:, None, None] * inside_y[None, :, None] * inside_z[None, None, :]
    centre_shift, width = (DEGREE + shift_value) / OPERATOR_SCALE - 1.0, DEGREE**0.5 / OPERATOR_SCALE
    to_power, constant, removed = basis_change(centre_shift, width)

    def centred(values, degree):
        weights = crop_margin(weight_pad, degree, BLOCK)
        result = stencil(values, weights, shift_value, BLOCK)
        return (result - centre_shift * crop_margin(values, 1, BLOCK)) * (1.0 / width)

    previous = padded
    current = centred(padded, 0) * crop_margin(inside, 1, BLOCK)
    powers = [crop_margin(current, POWERS - 1, BLOCK).reshape(size_x, size_y, size_z, BLOCK)]
    for degree in range(1, POWERS):
        following = centred(current, degree) - crop_margin(previous, 2, BLOCK)
        following = following * crop_margin(inside, degree + 1, BLOCK)
        previous, current = (current, following)
        powers.append(
            crop_margin(following, POWERS - 1 - degree, BLOCK).reshape(
                size_x, size_y, size_z, BLOCK
            )
        )
    columns = jnp.stack(powers, axis=3).reshape(cell_local, BLOCK * POWERS)
    joined = jnp.concatenate([basis_rows, columns], axis=1)
    sums = total(precise(joined.T, joined)) / cell_count
    inner, cross, square = sums[:BASIS, :BASIS], sums[:BASIS, BASIS:], sums[BASIS:, BASIS:]
    inner, cross, square = lax.optimization_barrier((inner, cross, square))
    defect = jnp.eye(BASIS, dtype=jnp.float32) - inner
    eye = jnp.eye(BLOCK, dtype=jnp.float32)
    start_defect = precise(defect, defect[:, BASIS - BLOCK :])
    both = cross + precise(defect, cross)
    both = lax.optimization_barrier(both)
    moved = lax.optimization_barrier(both - precise(start_defect, jnp.kron(removed, eye)))
    mix = jnp.kron(to_power, eye)
    start_unit = jnp.eye(BASIS, BLOCK, BLOCK - BASIS, dtype=jnp.float32)
    wide = jnp.concatenate([both, start_unit - start_defect], axis=1)
    projection = precise(wide, jnp.concatenate([mix, jnp.kron(constant, eye)], axis=0))
    gram = (
        square - precise(cross.T, moved) - precise(moved.T, cross - precise(inner, moved))
    )
    lower_factor = jnp.linalg.cholesky(gram)
    twice = columns - precise(basis_rows, moved)
    solved = jax.scipy.linalg.solve_triangular(lower_factor, twice.T, lower=True)
    new_basis = solved.T.reshape(size_x, size_y, size_z * BLOCK * POWERS)
    return (new_basis, projection, precise(lower_factor.T, mix))


def solution(mesh):
    return jax.shard_map(
        per_device,
        mesh=mesh,
        in_specs=(P("gx", "gy", "gz"), P(None, "gx", "gy", "gz"), P()),
        out_specs=(P("gx", "gy", "gz"), P(), P()),
        check_vma=False,
    )
```

```python
import functools
import math

import jax
import jax.numpy as jnp
from jax import lax
from jax.experimental import pallas as pl
from jax.experimental.pallas import tpu as pltpu
from jax.sharding import PartitionSpec as P

BLOCK = 32
POWERS = 4
BASIS = 96
WIDE = BLOCK * POWERS

PRECISE = lax.Precision.HIGHEST
OPERATOR_SCALE = 11.0
DEGREE = 6.0
LANES = 128
SUBLANES = 8
F32 = jnp.float32
BF16 = jnp.bfloat16
AXES = ("gx", "gy", "gz")


def lane_of(shape):
    return lax.broadcasted_iota(jnp.int32, shape, 1)


def row_of(shape):
    return lax.broadcasted_iota(jnp.int32, shape, 0)


def kernel_call(body, shapes, scratch=()):
    return pl.pallas_call(
        body,
        out_shape=[jax.ShapeDtypeStruct(shape, F32) for shape in shapes],
        scratch_shapes=list(scratch),
        compiler_params=pltpu.CompilerParams(vmem_limit_bytes=24 * 1024 * 1024),
    )


def pack_body(single, prior_ref, weights_ref, field_ref, *face_refs):
    size_x, size_y, width = field_ref.shape
    own = width - LANES
    size_z = own // BLOCK
    shape = (size_y, LANES)
    lane = lane_of(shape)
    first = lax.axis_index("gz") == 0
    for i in range(size_x):
        for q in range(own // LANES):
            tiles = [prior_ref[i, :, (3 * q + m) * LANES : (3 * q + m + 1) * LANES] for m in range(3)]
            low, high = pltpu.roll(tiles[0], 64, 1), pltpu.roll(tiles[2], 64, 1)
            value = jnp.where(lane < 64, jnp.where(lane < 32, low, tiles[1]), jnp.where(lane < 96, high, tiles[2]))
            field_ref[i, :, q * LANES : (q + 1) * LANES] = value
        pieces = [weights_ref[d, i] for d in range(3)]
        pieces.append(jnp.zeros((size_y, LANES - 3 * size_z), F32))
        weights = jnp.concatenate(pieces, axis=1)
        field_ref[i, :, own:] = weights
        low_face, high_face = field_ref[i, :, :LANES], field_ref[i, :, own - LANES : own]
        faces = [jnp.where(first, high_face, low_face)] if single else [high_face, low_face]
        for face_ref, face in zip(face_refs, faces):
            face_ref[i, :, :LANES] = face
            face_ref[i, :, LANES:] = weights


def widen_body(single, field_ref, *refs):
    halo_refs, (wide_ref, low_ref, high_ref) = refs[:-3], refs[-3:]
    size_x, size_y, width = field_ref.shape
    own = width - LANES
    size_z = own // BLOCK
    lane = lane_of((size_y, LANES))
    upper = (lane % size_z) < size_z // 2
    first = lax.axis_index("gz") == 0
    zero = jnp.zeros((size_y, LANES), F32)
    for i in range(size_x):
        if single:
            value, other = halo_refs[0][i, :, :LANES], halo_refs[0][i, :, LANES:]
            above, below = jnp.where(first, value, zero), jnp.where(first, zero, value)
            above_w, below_w = jnp.where(first, other, zero), jnp.where(first, zero, other)
        else:
            above, above_w = halo_refs[0][i, :, :LANES], halo_refs[0][i, :, LANES:]
            below, below_w = halo_refs[1][i, :, :LANES], halo_refs[1][i, :, LANES:]
        other = pltpu.roll(jnp.where(upper, above_w, below_w), 3 * size_z, 1)
        weights = jnp.where(lane < 3 * size_z, field_ref[i, :, own:], jnp.where(lane < 6 * size_z, other, zero))
        row = jnp.concatenate([field_ref[i, :, :own], above, below, weights], axis=1)
        wide_ref[i] = row
        low_ref[i] = row[:POWERS]
        high_ref[i] = row[size_y - POWERS :]


def lengthen_body(wide_ref, above_ref, below_ref, long_ref):
    size_x, size_y, _ = wide_ref.shape
    for i in range(size_x):
        long_ref[i, :size_y] = wide_ref[i]
        long_ref[i, size_y:] = jnp.concatenate([above_ref[i], below_ref[i]], axis=0)


def last_on(axis):
    return lax.axis_index(axis) == lax.axis_size(axis) - 1


def exact_dot(values, selector):
    high = values.astype(BF16)
    rest = values - high.astype(F32)
    middle = rest.astype(BF16)
    low = (rest - middle.astype(F32)).astype(BF16)
    dot = functools.partial(jnp.dot, preferred_element_type=F32)
    return dot(high, selector) + dot(middle, selector) + dot(low, selector)


def columns_body(size_z, own_ref, above_ref, below_ref, prior_ref, q_ref, s_ref, keep_ref, give_ref, coupling, diagonal, levels, sums):
    size_x, rows, width = own_ref.shape
    size_y = rows - 2 * POWERS
    field = width - LANES
    own = size_z * BLOCK
    planes = size_x + 2 * POWERS
    parts = (own_ref, above_ref, below_ref)

    def plane(p):
        if p < size_x:
            return own_ref, p
        return (above_ref, p - size_x) if p < size_x + POWERS else (below_ref, p - size_x - POWERS)

    weights = jnp.concatenate([ref[:, :, field:].reshape(-1, LANES) for ref in parts], axis=0)
    source = row_of((LANES, field))
    position = lane_of((LANES, field)) // BLOCK
    place = jnp.where(
        position < size_z,
        position,
        jnp.where(position < size_z + POWERS, position + 2 * size_z, position + 3 * size_z - 2 * POWERS),
    )
    unit = 1.0 / math.sqrt(DEGREE)
    for d in range(3):
        selector = (source == place + d * size_z).astype(F32).astype(BF16)
        spread = exact_dot(weights, selector) * unit
        coupling[d] = spread.reshape(planes, rows, field)
    row_last = (row_of((rows, field)) == size_y - 1) & last_on("gy")
    lane_last = (lane_of((rows, field)) // BLOCK == size_z - 1) & last_on("gz")

    near = lambda layers: [p for p in range(planes) if p < size_x + layers or p >= planes - layers]
    for p in near(POWERS - 1):
        x, y, z = (coupling[d, p] for d in range(3))
        x_low = coupling[0, (p - 1) % planes]
        diagonal[p] = x + x_low + (y + pltpu.roll(y, 1, 0)) + (z + pltpu.roll(z, BLOCK, 1)) - math.sqrt(DEGREE)
    for p in near(POWERS - 1):
        coupling[1, p] = jnp.where(row_last, 0.0, coupling[1, p])
        coupling[2, p] = jnp.where(lane_last, 0.0, coupling[2, p])
    coupling[0, size_x - 1] = jnp.where(last_on("gx"), 0.0, coupling[0, size_x - 1])

    def level(k, p):
        if k == 0:
            ref, at = plane(p)
            return ref[at, :, :field]
        return levels[k - 1, p]

    for k in range(1, POWERS + 1):
        for p in near(POWERS - k):
            value = level(k - 1, p)
            up, down = (p + 1) % planes, (p - 1) % planes
            x, y, z = (coupling[d, p] for d in range(3))
            total = diagonal[p] * value - x * level(k - 1, up) - coupling[0, down] * level(k - 1, down)
            total = total - y * pltpu.roll(value, rows - 1, 0) - pltpu.roll(y * value, 1, 0)
            total = total - z * pltpu.roll(value, field - BLOCK, 1) - pltpu.roll(z * value, BLOCK, 1)
            if k > 1:
                total = total - level(k - 2, p)
            if k == POWERS:
                levels[k - 1, p, :size_y, :own] = total[:size_y, :own]
            else:
                levels[k - 1, p] = total

    lane = lane_of((size_y, LANES))
    block = lane // BLOCK
    for i in range(size_x):
        for q in range(own // LANES):
            lanes = slice(q * LANES, (q + 1) * LANES)
            tiles = [levels[m, i, :size_y, lanes] for m in range(POWERS)]
            prior = [prior_ref[i, :, (3 * q + m) * LANES : (3 * q + m + 1) * LANES] for m in range(3)]
            prior_rows = [
                prior[0],
                jnp.where(lane < 32, pltpu.roll(prior[0], 32, 1), pltpu.roll(prior[1], 32, 1)),
                jnp.where(lane < 64, pltpu.roll(prior[1], 64, 1), pltpu.roll(prior[2], 64, 1)),
                pltpu.roll(prior[2], 96, 1),
            ]
            for r in range(4):
                moved = [pltpu.roll(tiles[m], (32 * (m - r)) % LANES, 1) if m != r else tiles[m] for m in range(POWERS)]
                row = jnp.where(block < 2, jnp.where(block < 1, moved[0], moved[1]), jnp.where(block < 3, moved[2], moved[3]))
                at = (i * size_z + 4 * q + r) * size_y
                s_ref[at : at + size_y] = row
                q_ref[at : at + size_y] = jnp.where(lane < BASIS, prior_rows[r], 0.0)

    contract = functools.partial(
        lax.dot_general, dimension_numbers=(((0,), (0,)), ((), ())), precision=PRECISE, preferred_element_type=F32
    )
    prior, columns = q_ref[...], s_ref[...]
    sums[:BASIS] = contract(prior, prior)[:BASIS]
    sums[BASIS : 2 * BASIS] = contract(prior, columns)[:BASIS]
    sums[2 * BASIS :] = contract(columns, columns)
    half = sums.shape[0] // 2
    odd = lax.axis_index("gx") % 2 == 1
    keep_ref[...] = jnp.where(odd, sums[half:], sums[:half])
    give_ref[...] = jnp.where(odd, sums[:half], sums[half:])


def split_rows(values):
    high = values.astype(BF16).astype(F32)
    rest = values - high
    middle = rest.astype(BF16).astype(F32)
    low = rest - middle
    left = jnp.concatenate([high, high, middle, high, low, middle], axis=0).astype(BF16)
    right = jnp.concatenate([high, middle, high, low, high, middle], axis=0).astype(BF16)
    return left, right


def factor_panel(left, right, column):
    size, count = left.shape
    entry = lambda i, j: jnp.broadcast_to(left[i : i + 1, column + j : column + j + 1], (size, count))
    a = {(i, j): entry(i, j) for i in range(size) for j in range(i, size)}
    row_a = [jnp.broadcast_to(left[i : i + 1, :], (size, count)) for i in range(size)]
    row_b = [jnp.broadcast_to(right[i : i + 1, :], (size, count)) for i in range(size)]
    for k in range(size):
        inverse = lax.rsqrt(a[k, k])
        row_a[k] = row_a[k] * inverse
        row_b[k] = row_b[k] * inverse
        scaled = {j: a[k, j] * inverse for j in range(k + 1, size)}
        for i in range(k + 1, size):
            for j in range(i, size):
                a[i, j] = a[i, j] - scaled[i] * scaled[j]
            row_a[i] = row_a[i] - scaled[i] * row_a[k]
            row_b[i] = row_b[i] - scaled[i] * row_b[k]
    sub = row_of((size, count))
    out_a, out_b = row_a[0], row_b[0]
    for i in range(1, size):
        out_a, out_b = jnp.where(sub == i, row_a[i], out_a), jnp.where(sub == i, row_b[i], out_b)
    return out_a, out_b


def factor(joined, upper, inverse):
    count = upper.shape[0]
    for start in range(0, count, SUBLANES):
        stop = start + SUBLANES
        out_a, out_b = factor_panel(joined[start:stop, :count], joined[start:stop, count:], start)
        shape = (SUBLANES, count)
        upper[start:stop] = jnp.where(lane_of(shape) >= row_of(shape) + start, out_a, 0.0)
        inverse[start:stop] = out_b
        if stop < count:
            left, right = split_rows(jnp.concatenate([out_a, out_b], axis=1))
            update = lax.dot_general(
                left[:, :count], right, (((0,), (0,)), ((), ())), preferred_element_type=F32
            )
            joined[stop:] = joined[stop:] - update[stop:]


def basis_change(centre, width):
    def apply_a(c):
        up = [0.0] + [width * v for v in c[:-1]]
        down = [width * v for v in c[1:]] + [0.0]
        return [centre * v + u + d for v, u, d in zip(c, up, down)]

    def apply_x(c):
        out = [0.0] * len(c)
        out[1] = out[1] + c[0]
        for k in range(1, len(c)):
            if k + 1 < len(c):
                out[k + 1] = out[k + 1] + 0.5 * c[k]
            out[k - 1] = out[k - 1] + 0.5 * c[k]
        return [(o - centre * v) * (1.0 / width) for o, v in zip(out, c)]

    one = centre * 0.0 + 1.0
    t = [[one] + [0.0] * POWERS]
    s = [[one] + [0.0] * POWERS]
    t.append(apply_a(t[0]))
    s.append(apply_x(s[0]))
    for _ in range(1, POWERS):
        t.append([2.0 * v - w for v, w in zip(apply_a(t[-1]), t[-2])])
        s.append([v - w for v, w in zip(apply_x(s[-1]), s[-2])])
    return t, s


def per_block(values):
    block = lane_of((SUBLANES, WIDE)) // BLOCK
    out = jnp.zeros((SUBLANES, WIDE), F32)
    for k, value in enumerate(values):
        out = jnp.where(block == k, value, out)
    return out[:1]


def finish_body(scale, shift_ref, q_ref, s_ref, mine_ref, other_ref, basis_ref, projection_ref, triangle_ref, sums, joined, upper, inverse):
    size_x, size_y, width = basis_ref.shape
    size_z = width // WIDE
    half = mine_ref.shape[0]
    odd = lax.axis_index("gx") % 2 == 1
    sums[:half] = jnp.where(odd, other_ref[...], mine_ref[...]) * scale
    sums[half:] = jnp.where(odd, mine_ref[...], other_ref[...]) * scale
    dot = functools.partial(jnp.dot, precision=PRECISE, preferred_element_type=F32)

    centre, spread = (DEGREE + shift_ref[0]) * (1.0 / OPERATOR_SCALE) - 1.0, math.sqrt(DEGREE) / OPERATOR_SCALE
    t, s = basis_change(centre, spread)
    constant = per_block([t[k][0] for k in range(1, POWERS + 1)])
    removed = per_block([-s[k][0] for k in range(1, POWERS + 1)])
    mixes = [
        per_block([t[k][k - m] if k > m else 0.0 for k in range(1, POWERS + 1)]) for m in range(POWERS)
    ]

    def to_powers(values):
        total = values * mixes[0]
        for m in range(1, POWERS):
            total = total + pltpu.roll(values, m * BLOCK, 1) * mixes[m]
        return total

    inner, cross = sums[:BASIS], sums[BASIS : 2 * BASIS]
    shape = inner.shape
    row, lane = row_of(shape), lane_of(shape)
    block = lane // BLOCK
    defect = jnp.where(row == lane, 1.0, 0.0) - inner
    first = (BASIS - BLOCK) // BLOCK
    copies = [pltpu.roll(defect, ((k - first) * BLOCK) % WIDE, 1) if k != first else defect for k in range(POWERS)]
    start = jnp.where(block < 2, jnp.where(block < 1, copies[0], copies[1]), jnp.where(block < 3, copies[2], copies[3]))
    start_defect = dot(defect[:, :BASIS], start)
    both = cross + dot(defect[:, :BASIS], cross)
    moved = both - start_defect * removed
    start_unit = jnp.where(row - (BASIS - BLOCK) == lane - block * BLOCK, 1.0, 0.0)
    projection_ref[...] = to_powers(both) + (start_unit - start_defect) * constant
    left = cross - dot(inner[:, :BASIS], moved)
    product = lax.dot_general(
        jnp.concatenate([cross, moved], axis=0),
        jnp.concatenate([moved, left], axis=0),
        (((0,), (0,)), ((), ())),
        precision=PRECISE,
        preferred_element_type=F32,
    )
    joined[:, :WIDE] = sums[2 * BASIS :] - product
    shape = (WIDE, WIDE)
    joined[:, WIDE:] = jnp.where(row_of(shape) == lane_of(shape), 1.0, 0.0)
    padded = jnp.concatenate([moved, jnp.zeros((WIDE - BASIS, WIDE), F32)], axis=0)
    twice = s_ref[...] - dot(q_ref[...], padded)
    factor(joined, upper, inverse)
    triangle_ref[...] = to_powers(upper[...])
    new_basis = lax.dot_general(
        twice, inverse[...], (((1,), (1,)), ((), ())), precision=PRECISE, preferred_element_type=F32
    )
    for i in range(size_x):
        for k in range(size_z):
            at = (i * size_z + k) * size_y
            basis_ref[i, :, k * WIDE : (k + 1) * WIDE] = new_basis[at : at + size_y]


def swap(values, axis, step):
    count = lax.axis_size(axis)
    return lax.ppermute(values, axis, [(i, i ^ step) for i in range(count)])


def to_next(values, axis):
    return lax.ppermute(values, axis, [(i, i + 1) for i in range(lax.axis_size(axis) - 1)])


def to_previous(values, axis):
    return lax.ppermute(values, axis, [(i + 1, i) for i in range(lax.axis_size(axis) - 1)])


def doublings(axis):
    count = lax.axis_size(axis)
    return [1 << k for k in range(count.bit_length() - 1)]


def per_device(prior_basis, edge_weights, spectral_shift):
    size_x, size_y, _ = prior_basis.shape
    size_z = prior_basis.shape[2] // BASIS
    own = size_z * BLOCK
    single = lax.axis_size("gz") == 2
    cell_local = size_x * size_y * size_z
    cell_count = cell_local
    for axis in AXES:
        cell_count = cell_count * lax.axis_size(axis)

    face = (size_x, size_y, 2 * LANES)
    field, *faces = kernel_call(
        functools.partial(pack_body, single), [(size_x, size_y, own + LANES)] + [face] * (1 if single else 2)
    )(prior_basis, edge_weights)
    if single:
        halos = [swap(faces[0], "gz", 1)]
    else:
        halos = [to_previous(faces[1], "gz"), to_next(faces[0], "gz")]
    width = own + 3 * LANES
    wide, low, high = kernel_call(
        functools.partial(widen_body, single),
        [(size_x, size_y, width)] + [(size_x, POWERS, width)] * 2,
    )(field, *halos)
    below, above = to_next(high, "gy"), to_previous(low, "gy")
    (long,) = kernel_call(lengthen_body, [(size_x, size_y + 2 * POWERS, width)])(wide, above, below)
    below, above = to_next(long[-POWERS:], "gx"), to_previous(long[:POWERS], "gx")

    rows, planes, lanes = size_y + 2 * POWERS, size_x + 2 * POWERS, own + 2 * LANES
    sum_rows = 2 * BASIS + WIDE
    half = (sum_rows // 2, WIDE)
    prior_rows, columns, keep, give = kernel_call(
        functools.partial(columns_body, size_z),
        [(cell_local, LANES), (cell_local, WIDE), half, half],
        [
            pltpu.VMEM((3, planes, rows, lanes), F32),
            pltpu.VMEM((planes, rows, lanes), F32),
            pltpu.VMEM((POWERS, planes, rows, lanes), F32),
            pltpu.VMEM((sum_rows, WIDE), F32),
        ],
    )(long, above, below, prior_basis)

    total = keep + swap(give, "gx", 1)
    for axis in ("gx", "gz", "gy"):
        for step in doublings(axis):
            if (axis, step) != ("gx", 1):
                total = total + swap(total, axis, step)
    other = swap(total, "gx", 1)

    new_basis, projection, triangle = pl.pallas_call(
        functools.partial(finish_body, 1.0 / cell_count),
        in_specs=[pl.BlockSpec(memory_space=pltpu.SMEM)] + [pl.BlockSpec(memory_space=pltpu.VMEM)] * 4,
        out_shape=[
            jax.ShapeDtypeStruct((size_x, size_y, size_z * WIDE), F32),
            jax.ShapeDtypeStruct((BASIS, WIDE), F32),
            jax.ShapeDtypeStruct((WIDE, WIDE), F32),
        ],
        scratch_shapes=[
            pltpu.VMEM((sum_rows, WIDE), F32),
            pltpu.VMEM((WIDE, 2 * WIDE), F32),
            pltpu.VMEM((WIDE, WIDE), F32),
            pltpu.VMEM((WIDE, WIDE), F32),
        ],
        compiler_params=pltpu.CompilerParams(vmem_limit_bytes=24 * 1024 * 1024),
    )(spectral_shift, prior_rows, columns, total, other)
    return new_basis, projection, triangle


def solution(mesh):
    return jax.shard_map(
        per_device,
        mesh=mesh,
        in_specs=(P("gx", "gy", "gz"), P(None, "gx", "gy", "gz"), P()),
        out_specs=(P("gx", "gy", "gz"), P(), P()),
        check_vma=False,
    )
```

```python
import functools
import math

import jax
import jax.numpy as jnp
from jax import lax
from jax.experimental import pallas as pl
from jax.experimental.pallas import tpu as pltpu
from jax.sharding import PartitionSpec as P

BLOCK = 32
POWERS = 4
BASIS = 96
WIDE = BLOCK * POWERS

PRECISE = lax.Precision.HIGHEST
OPERATOR_SCALE = 11.0
DEGREE = 6.0
LANES = 128
SUBLANES = 8
F32 = jnp.float32
BF16 = jnp.bfloat16
AXES = ("gx", "gy", "gz")


def lane_of(shape):
    return lax.broadcasted_iota(jnp.int32, shape, 1)


def row_of(shape):
    return lax.broadcasted_iota(jnp.int32, shape, 0)


def kernel_call(body, shapes, scratch=(), in_specs=None, cost=None, limit=24 * 1024 * 1024):
    options = {} if in_specs is None else {"in_specs": in_specs}
    return pl.pallas_call(
        body,
        out_shape=[jax.ShapeDtypeStruct(shape, F32) for shape in shapes],
        scratch_shapes=list(scratch),
        compiler_params=pltpu.CompilerParams(vmem_limit_bytes=limit),
        cost_estimate=cost,
        **options,
    )


def even_on(axis):
    return lax.axis_index(axis) % 2 == 0


def pick(even, first, second):
    return jnp.where(even, first, second)


def pack_body(prior_hbm, weights_hbm, field_ref, *refs):
    face_refs, (prior_ref, weights_ref, prior_sem, weights_sem) = refs[:-4], refs[-4:]
    size_x, size_y, width = field_ref.shape
    weights_copy = pltpu.make_async_copy(weights_hbm, weights_ref, weights_sem)
    copies = [pltpu.make_async_copy(prior_hbm.at[i], prior_ref.at[i], prior_sem.at[i]) for i in range(size_x)]
    weights_copy.start()
    for copy in copies:
        copy.start()
    own = width - LANES
    size_z = own // BLOCK
    shape = (size_y, LANES)
    lane = lane_of(shape)
    even = even_on("gz")
    weights_copy.wait()
    for i in range(size_x):
        pieces = [weights_ref[d, i] for d in range(3)]
        pieces.append(jnp.zeros((size_y, LANES - 3 * size_z), F32))
        weights = jnp.concatenate(pieces, axis=1)
        field_ref[i, :, own:] = weights
        for face_ref in face_refs:
            face_ref[i, :, LANES:] = weights
    for i in range(size_x):
        copies[i].wait()
        values = []
        for q in range(own // LANES):
            tiles = [prior_ref[i, :, (3 * q + m) * LANES : (3 * q + m + 1) * LANES] for m in range(3)]
            low, high = pltpu.roll(tiles[0], 64, 1), pltpu.roll(tiles[2], 64, 1)
            value = jnp.where(lane < 64, jnp.where(lane < 32, low, tiles[1]), jnp.where(lane < 96, high, tiles[2]))
            field_ref[i, :, q * LANES : (q + 1) * LANES] = value
            values.append(value)
        faces = [pick(even, values[-1], values[0]), pick(even, values[0], values[-1])]
        for face_ref, face in zip(face_refs, faces):
            face_ref[i, :, :LANES] = face


def widen_body(field_ref, *refs):
    halo_refs, (wide_ref, *face_refs) = refs[:-3], refs[-3:]
    size_x, size_y, width = field_ref.shape
    own = width - LANES
    size_z = own // BLOCK
    lane = lane_of((size_y, LANES))
    upper = (lane % size_z) < size_z // 2
    even, even_y = even_on("gz"), even_on("gy")
    zero = jnp.zeros((size_y, LANES), F32)
    for i in range(size_x):
        values = [ref[i, :, :LANES] for ref in halo_refs] + [zero, zero]
        others = [ref[i, :, LANES:] for ref in halo_refs] + [zero, zero]
        above, below = pick(even, values[0], values[1]), pick(even, values[1], values[0])
        above_w, below_w = pick(even, others[0], others[1]), pick(even, others[1], others[0])
        other = pltpu.roll(jnp.where(upper, above_w, below_w), 3 * size_z, 1)
        weights = jnp.where(lane < 3 * size_z, field_ref[i, :, own:], jnp.where(lane < 6 * size_z, other, zero))
        row = jnp.concatenate([field_ref[i, :, :own], above, below, weights], axis=1)
        wide_ref[i] = row
        low, high = row[:POWERS], row[size_y - POWERS :]
        face_refs[0][i] = pick(even_y, high, low)
        face_refs[1][i] = pick(even_y, low, high)


def lengthen_body(wide_ref, first_ref, second_ref, long_ref, *rest_refs):
    size_x, size_y, width = wide_ref.shape
    even, even_x = even_on("gy"), even_on("gx")
    rest = []
    for i in range(size_x):
        wide = wide_ref[i]
        long_ref[i, :size_y] = wide
        first, second = first_ref[i], second_ref[i]
        halo = jnp.concatenate([pick(even, first, second), pick(even, second, first)], axis=0)
        long_ref[i, size_y:] = halo
        side = wide[:, width - 3 * LANES :]
        pieces = [side[row : row + SUBLANES] for row in range(0, size_y, SUBLANES)]
        rest.append(jnp.concatenate(pieces + [halo], axis=1))
    for at in range(POWERS - 1):
        low, high = rest[at], rest[size_x - POWERS + 1 + at]
        rest_refs[0][at] = pick(even_x, high, low)
        rest_refs[1][at] = pick(even_x, low, high)


def contract(left, right):
    return lax.dot_general(
        left, right, (((0,), (0,)), ((), ())), precision=PRECISE, preferred_element_type=F32
    )


def prior_body(prior_ref, q_ref, inner_ref):
    size_x, size_y, width = prior_ref.shape
    size_z = width // BASIS
    lane = lane_of((size_y, LANES))
    for i in range(size_x):
        for q in range(width // (3 * LANES)):
            prior = [prior_ref[i, :, (3 * q + m) * LANES : (3 * q + m + 1) * LANES] for m in range(3)]
            rows = [
                prior[0],
                jnp.where(lane < 32, pltpu.roll(prior[0], 32, 1), pltpu.roll(prior[1], 32, 1)),
                jnp.where(lane < 64, pltpu.roll(prior[1], 64, 1), pltpu.roll(prior[2], 64, 1)),
                pltpu.roll(prior[2], 96, 1),
            ]
            for r in range(4):
                at = (i * size_z + 4 * q + r) * size_y
                q_ref[at : at + size_y] = jnp.where(lane < BASIS, rows[r], 0.0)
    rows = q_ref[...]
    inner_ref[...] = contract(rows, rows)[:BASIS]


def last_on(axis):
    return lax.axis_index(axis) == lax.axis_size(axis) - 1


def exact_dot(values, selector):
    high = values.astype(BF16)
    rest = values - high.astype(F32)
    middle = rest.astype(BF16)
    low = (rest - middle.astype(F32)).astype(BF16)
    dot = functools.partial(jnp.dot, preferred_element_type=F32)
    return dot(high, selector) + dot(middle, selector) + dot(low, selector)


def columns_body(size_z, own_ref, near_ref, far_ref, near_rest_ref, far_rest_ref, q_ref, inner_ref, s_ref, keep_ref, give_ref, joined, coupling, diagonal, levels, sums):
    size_x, rows, width = own_ref.shape
    size_y = rows - 2 * POWERS
    field = width - LANES
    own = size_z * BLOCK
    planes = size_x + 2 * POWERS
    even = even_on("gx")
    joined[:size_x] = own_ref[...]
    for at in range(POWERS):
        near, far = near_ref[at], far_ref[at]
        above, below = size_x + at, size_x + POWERS + at
        near_high, far_high = near_ref[near_ref.shape[0] - POWERS + at], far_ref[near_ref.shape[0] - POWERS + at]
        for p, value in ((above, pick(even, near, far)), (below, pick(even, far_high, near_high))):
            joined[p, :size_y, :own] = value[:, :own]
            joined[p, :size_y, field:] = value[:, own:]
    zero = jnp.zeros((size_y, 2 * LANES), F32)
    for p in (size_x + POWERS - 1, size_x + POWERS):
        joined[p, :size_y, own:field] = zero
        joined[p, size_y:] = jnp.zeros((2 * POWERS, width), F32)
    for at in range(POWERS - 1):
        near, far = near_rest_ref[at], far_rest_ref[at]
        for p, value in ((size_x + at, pick(even, near, far)), (size_x + POWERS + 1 + at, pick(even, far, near))):
            for part in range(size_y // SUBLANES):
                lanes = slice(3 * part * LANES, 3 * (part + 1) * LANES)
                joined[p, part * SUBLANES : (part + 1) * SUBLANES, own:] = value[:, lanes]
            joined[p, size_y:] = value[:, 3 * (size_y // SUBLANES) * LANES :]

    weights = joined[:, :, field:].reshape(-1, LANES)
    source = row_of((LANES, field))
    position = lane_of((LANES, field)) // BLOCK
    place = jnp.where(
        position < size_z,
        position,
        jnp.where(position < size_z + POWERS, position + 2 * size_z, position + 3 * size_z - 2 * POWERS),
    )
    unit = 1.0 / math.sqrt(DEGREE)
    for d in range(3):
        selector = (source == place + d * size_z).astype(F32).astype(BF16)
        spread = exact_dot(weights, selector) * unit
        coupling[d] = spread.reshape(planes, rows, field)
    row_last = (row_of((rows, field)) == size_y - 1) & last_on("gy")
    lane_last = (lane_of((rows, field)) // BLOCK == size_z - 1) & last_on("gz")

    near = lambda layers: [p for p in range(planes) if p < size_x + layers or p >= planes - layers]
    for p in near(POWERS - 1):
        x, y, z = (coupling[d, p] for d in range(3))
        x_low = coupling[0, (p - 1) % planes]
        diagonal[p] = x + x_low + (y + pltpu.roll(y, 1, 0)) + (z + pltpu.roll(z, BLOCK, 1)) - math.sqrt(DEGREE)
    for p in near(POWERS - 1):
        coupling[1, p] = jnp.where(row_last, 0.0, coupling[1, p])
        coupling[2, p] = jnp.where(lane_last, 0.0, coupling[2, p])
    coupling[0, size_x - 1] = jnp.where(last_on("gx"), 0.0, coupling[0, size_x - 1])

    def level(k, p):
        return joined[p, :, :field] if k == 0 else levels[k - 1, p]

    for k in range(1, POWERS + 1):
        for p in near(POWERS - k):
            value = level(k - 1, p)
            up, down = (p + 1) % planes, (p - 1) % planes
            x, y, z = (coupling[d, p] for d in range(3))
            total = diagonal[p] * value - x * level(k - 1, up) - coupling[0, down] * level(k - 1, down)
            total = total - y * pltpu.roll(value, rows - 1, 0) - pltpu.roll(y * value, 1, 0)
            total = total - z * pltpu.roll(value, field - BLOCK, 1) - pltpu.roll(z * value, BLOCK, 1)
            if k > 1:
                total = total - level(k - 2, p)
            if k == POWERS:
                levels[k - 1, p, :size_y, :own] = total[:size_y, :own]
            else:
                levels[k - 1, p] = total

    lane = lane_of((size_y, LANES))
    block = lane // BLOCK
    for i in range(size_x):
        for q in range(own // LANES):
            tiles = [levels[m, i, :size_y, q * LANES : (q + 1) * LANES] for m in range(POWERS)]
            for r in range(4):
                moved = [pltpu.roll(tiles[m], (32 * (m - r)) % LANES, 1) if m != r else tiles[m] for m in range(POWERS)]
                at = (i * size_z + 4 * q + r) * size_y
                s_ref[at : at + size_y] = by_block(block, moved)

    columns = s_ref[...]
    sums[:BASIS] = contract(q_ref[...], columns)[:BASIS]
    last = contract(columns[:, WIDE - BLOCK :], columns)
    inner = inner_ref[...]
    block = lane_of((BLOCK, LANES)) // BLOCK
    turned = pltpu.roll(last, 96, 1)
    sums[BASIS : BASIS + 32] = jnp.where(block < 3, inner[:32], turned)
    sums[BASIS + 32 : BASIS + 64] = by_block(block, [turned, inner[32:64], inner[32:64], pltpu.roll(last, 32, 1)])
    block = block[:16]
    sums[BASIS + 64 :] = by_block(
        block,
        [pltpu.roll(inner[64:80], 64, 1), pltpu.roll(inner[80:96], 96, 1), pltpu.roll(last[:16], 96, 1), last[16:]],
    )
    half = sums.shape[0] // 2
    even = even_on("gx")
    keep_ref[...] = pick(even, sums[:half], sums[half:])
    give_ref[...] = pick(even, sums[half:], sums[:half])


def by_block(block, values):
    return jnp.where(
        block < 2, jnp.where(block < 1, values[0], values[1]), jnp.where(block < 3, values[2], values[3])
    )


def unpack(sums):
    cross = sums[:BASIS]
    top, middle, tail = sums[BASIS : BASIS + 32], sums[BASIS + 32 : BASIS + 64], sums[BASIS + 64 : BASIS + 80]
    block = lane_of((BLOCK, LANES)) // BLOCK
    corner = jnp.concatenate([pltpu.roll(tail, 64, 1), pltpu.roll(tail, 32, 1)], axis=0)
    moment = jnp.concatenate([tail, pltpu.roll(tail, 96, 1)], axis=0)
    last = jnp.concatenate([pltpu.roll(tail, 32, 1), tail], axis=0)
    upper = jnp.concatenate([top, middle, corner, jnp.zeros((BLOCK, LANES), F32)], axis=0)
    row, lane = row_of((BASIS, LANES)) // BLOCK, lane_of((BASIS, LANES)) // BLOCK
    inner = jnp.where(row <= lane, upper[:BASIS], jnp.transpose(upper)[:BASIS])
    inner = jnp.where(lane < BASIS // BLOCK, inner, 0.0)
    moments = cross[BASIS - BLOCK :]
    half = pltpu.roll(moments, 64, 1)
    first = jnp.where(block == 0, moment, pltpu.roll(moments, 32, 1)) + pltpu.roll(moments, 96, 1)
    first = jnp.where(block == 3, top, first)
    second = jnp.where(block == 2, half + pltpu.roll(top, 96, 1), pltpu.roll(moment, 32, 1) + moments + half)
    second = jnp.where(block == 3, pltpu.roll(middle, 96, 1), second)
    third = jnp.where(block == 3, middle, corner + pltpu.roll(middle, 64, 1))
    return inner, cross, jnp.concatenate([first, second, third, last], axis=0)


def split_rows(values):
    high = values.astype(BF16).astype(F32)
    rest = values - high
    middle = rest.astype(BF16).astype(F32)
    low = rest - middle
    left = jnp.concatenate([high, high, middle, high, low, middle], axis=0).astype(BF16)
    right = jnp.concatenate([high, middle, high, low, high, middle], axis=0).astype(BF16)
    return left, right


def factor_panel(left, right, column):
    size, count = left.shape
    entry = lambda i, j: jnp.broadcast_to(left[i : i + 1, column + j : column + j + 1], (size, count))
    a = {(i, j): entry(i, j) for i in range(size) for j in range(i, size)}
    row_a = [jnp.broadcast_to(left[i : i + 1, :], (size, count)) for i in range(size)]
    row_b = [jnp.broadcast_to(right[i : i + 1, :], (size, count)) for i in range(size)]
    for k in range(size):
        inverse = lax.rsqrt(a[k, k])
        row_a[k] = row_a[k] * inverse
        row_b[k] = row_b[k] * inverse
        scaled = {j: a[k, j] * inverse for j in range(k + 1, size)}
        for i in range(k + 1, size):
            for j in range(i, size):
                a[i, j] = a[i, j] - scaled[i] * scaled[j]
            row_a[i] = row_a[i] - scaled[i] * row_a[k]
            row_b[i] = row_b[i] - scaled[i] * row_b[k]
    sub = row_of((size, count))
    out_a, out_b = row_a[0], row_b[0]
    for i in range(1, size):
        out_a, out_b = jnp.where(sub == i, row_a[i], out_a), jnp.where(sub == i, row_b[i], out_b)
    return out_a, out_b


def factor(joined, upper, inverse):
    count = upper.shape[0]
    for start in range(0, count, SUBLANES):
        stop = start + SUBLANES
        out_a, out_b = factor_panel(joined[start:stop, :count], joined[start:stop, count:], start)
        shape = (SUBLANES, count)
        out_a = jnp.where(lane_of(shape) >= row_of(shape) + start, out_a, 0.0)
        upper[start:stop] = out_a
        inverse[start:stop] = out_b
        if stop < count:
            left, right = split_rows(jnp.concatenate([out_a, out_b], axis=1))
            update = lax.dot_general(
                left[:, :count], right, (((0,), (0,)), ((), ())), preferred_element_type=F32
            )
            joined[stop:] = joined[stop:] - update[stop:]


def basis_change(centre, width):
    def apply_a(c):
        up = [0.0] + [width * v for v in c[:-1]]
        down = [width * v for v in c[1:]] + [0.0]
        return [centre * v + u + d for v, u, d in zip(c, up, down)]

    def apply_x(c):
        out = [0.0] * len(c)
        out[1] = out[1] + c[0]
        for k in range(1, len(c)):
            if k + 1 < len(c):
                out[k + 1] = out[k + 1] + 0.5 * c[k]
            out[k - 1] = out[k - 1] + 0.5 * c[k]
        return [(o - centre * v) * (1.0 / width) for o, v in zip(out, c)]

    one = centre * 0.0 + 1.0
    t = [[one] + [0.0] * POWERS]
    s = [[one] + [0.0] * POWERS]
    t.append(apply_a(t[0]))
    s.append(apply_x(s[0]))
    for _ in range(1, POWERS):
        t.append([2.0 * v - w for v, w in zip(apply_a(t[-1]), t[-2])])
        s.append([v - w for v, w in zip(apply_x(s[-1]), s[-2])])
    return t, s


def per_block(values):
    block = lane_of((SUBLANES, WIDE)) // BLOCK
    out = jnp.zeros((SUBLANES, WIDE), F32)
    for k, value in enumerate(values):
        out = jnp.where(block == k, value, out)
    return out[:1]


def finish_body(scale, shift_ref, q_ref, s_ref, mine_ref, other_ref, basis_ref, projection_ref, triangle_ref, joined, upper, inverse):
    size_x, size_y, width = basis_ref.shape
    size_z = width // WIDE
    even = even_on("gx")
    mine, other = mine_ref[...] * scale, other_ref[...] * scale
    sums = jnp.concatenate([pick(even, mine, other), pick(even, other, mine)], axis=0)
    dot = functools.partial(jnp.dot, precision=PRECISE, preferred_element_type=F32)

    centre, spread = (DEGREE + shift_ref[0]) * (1.0 / OPERATOR_SCALE) - 1.0, math.sqrt(DEGREE) / OPERATOR_SCALE
    t, s = basis_change(centre, spread)
    constant = per_block([t[k][0] for k in range(1, POWERS + 1)])
    removed = per_block([-s[k][0] for k in range(1, POWERS + 1)])
    mixes = [
        per_block([t[k][k - m] if k > m else 0.0 for k in range(1, POWERS + 1)]) for m in range(POWERS)
    ]

    def to_powers(values):
        total = values * mixes[0]
        for m in range(1, POWERS):
            total = total + pltpu.roll(values, m * BLOCK, 1) * mixes[m]
        return total

    inner, cross, square = unpack(sums)
    shape = inner.shape
    row, lane = row_of(shape), lane_of(shape)
    block = lane // BLOCK
    defect = jnp.where(row == lane, 1.0, 0.0) - inner
    first = (BASIS - BLOCK) // BLOCK
    copies = [pltpu.roll(defect, ((k - first) * BLOCK) % WIDE, 1) if k != first else defect for k in range(POWERS)]
    start = jnp.where(block < 2, jnp.where(block < 1, copies[0], copies[1]), jnp.where(block < 3, copies[2], copies[3]))
    start_defect = dot(defect[:, :BASIS], start)
    both = cross + dot(defect[:, :BASIS], cross)
    moved = both - start_defect * removed
    start_unit = jnp.where(row - (BASIS - BLOCK) == lane - block * BLOCK, 1.0, 0.0)
    projection_ref[...] = to_powers(both) + (start_unit - start_defect) * constant
    left = cross - dot(inner[:, :BASIS], moved)
    product = contract(jnp.concatenate([cross, moved], axis=0), jnp.concatenate([moved, left], axis=0))
    joined[:, :WIDE] = square - product
    shape = (WIDE, WIDE)
    joined[:, WIDE:] = jnp.where(row_of(shape) == lane_of(shape), 1.0, 0.0)
    padded = jnp.concatenate([moved, jnp.zeros((WIDE - BASIS, WIDE), F32)], axis=0)
    twice = s_ref[...] - dot(q_ref[...], padded)
    factor(joined, upper, inverse)
    triangle_ref[...] = to_powers(upper[...])
    new_basis = lax.dot_general(
        twice, inverse[...], (((1,), (1,)), ((), ())), precision=PRECISE, preferred_element_type=F32
    )
    for i in range(size_x):
        for k in range(size_z):
            at = (i * size_z + k) * size_y
            basis_ref[i, :, k * WIDE : (k + 1) * WIDE] = new_basis[at : at + size_y]


def swap(values, axis, step):
    count = lax.axis_size(axis)
    return lax.ppermute(values, axis, [(i, i ^ step) for i in range(count)])


def exchange(first, second, axis):
    count = lax.axis_size(axis)
    pairs = [(i, i ^ 1) for i in range(count) if i ^ 1 < count]
    across = [(i, j) for k in range(1, count - 1, 2) for i, j in ((k, k + 1), (k + 1, k))]
    got = [lax.ppermute(first, axis, pairs)] if pairs else []
    return got + ([lax.ppermute(second, axis, across)] if across else [])


def filled(halos, like):
    return halos + [jnp.zeros_like(like)] * (2 - len(halos))


def doublings(axis):
    count = lax.axis_size(axis)
    return [1 << k for k in range(count.bit_length() - 1)]


def per_device(prior_basis, edge_weights, spectral_shift):
    size_x, size_y, _ = prior_basis.shape
    size_z = prior_basis.shape[2] // BASIS
    own = size_z * BLOCK
    cell_local = size_x * size_y * size_z
    cell_count = cell_local
    for axis in AXES:
        cell_count = cell_count * lax.axis_size(axis)

    hbm = pl.BlockSpec(memory_space=pltpu.HBM)
    faces = min(lax.axis_size("gz") - 1, 2)
    field, *faces = kernel_call(
        pack_body,
        [(size_x, size_y, own + LANES)] + [(size_x, size_y, 2 * LANES)] * faces,
        [
            pltpu.VMEM(prior_basis.shape, F32),
            pltpu.VMEM(edge_weights.shape, F32),
            pltpu.SemaphoreType.DMA((size_x,)),
            pltpu.SemaphoreType.DMA(()),
        ],
        [hbm, hbm],
    )(*(pltpu.with_memory_space_constraint(array, pltpu.HBM) for array in (prior_basis, edge_weights)))
    halos = exchange(faces[0], faces[-1], "gz") if faces else []
    planes_x = filled(exchange(field, field, "gx"), field)
    prior_rows, inner = kernel_call(
        prior_body,
        [(cell_local, LANES), (BASIS, LANES)],
        cost=pl.CostEstimate(flops=6 * 2 * cell_local * LANES * LANES, bytes_accessed=4 * prior_basis.size, transcendentals=0),
    )(prior_basis)
    width = own + 3 * LANES
    wide, first, second = kernel_call(
        widen_body, [(size_x, size_y, width)] + [(size_x, POWERS, width)] * 2
    )(field, *halos)
    halos = filled(exchange(first, second, "gy"), first)
    rest = (POWERS - 1, SUBLANES, 3 * LANES * (size_y // SUBLANES) + width)
    long, first, second = kernel_call(lengthen_body, [(size_x, size_y + 2 * POWERS, width), rest, rest])(wide, *halos)
    rests = filled(exchange(first, second, "gx"), first)

    rows, planes, lanes = size_y + 2 * POWERS, size_x + 2 * POWERS, own + 2 * LANES
    sum_rows = BASIS + 80
    half = (sum_rows // 2, WIDE)
    columns, keep, give = kernel_call(
        functools.partial(columns_body, size_z),
        [(cell_local, WIDE), half, half],
        [
            pltpu.VMEM((planes, rows, width), F32),
            pltpu.VMEM((3, planes, rows, lanes), F32),
            pltpu.VMEM((planes, rows, lanes), F32),
            pltpu.VMEM((POWERS, planes, rows, lanes), F32),
            pltpu.VMEM((sum_rows, WIDE), F32),
        ],
    )(long, *planes_x, *rests, prior_rows, inner)

    total = keep + swap(give, "gx", 1)
    for axis in ("gx", "gz", "gy"):
        for step in doublings(axis):
            if (axis, step) != ("gx", 1):
                total = total + swap(total, axis, step)
    other = swap(total, "gx", 1)

    new_basis, projection, triangle = pl.pallas_call(
        functools.partial(finish_body, 1.0 / cell_count),
        in_specs=[pl.BlockSpec(memory_space=pltpu.SMEM)] + [pl.BlockSpec(memory_space=pltpu.VMEM)] * 4,
        out_shape=[
            jax.ShapeDtypeStruct((size_x, size_y, size_z * WIDE), F32),
            jax.ShapeDtypeStruct((BASIS, WIDE), F32),
            jax.ShapeDtypeStruct((WIDE, WIDE), F32),
        ],
        scratch_shapes=[
            pltpu.VMEM((WIDE, 2 * WIDE), F32),
            pltpu.VMEM((WIDE, WIDE), F32),
            pltpu.VMEM((WIDE, WIDE), F32),
        ],
        compiler_params=pltpu.CompilerParams(vmem_limit_bytes=24 * 1024 * 1024),
    )(spectral_shift, prior_rows, columns, total, other)
    return new_basis, projection, triangle


def solution(mesh):
    return jax.shard_map(
        per_device,
        mesh=mesh,
        in_specs=(P("gx", "gy", "gz"), P(None, "gx", "gy", "gz"), P()),
        out_specs=(P("gx", "gy", "gz"), P(), P()),
        check_vma=False,
    )
```

```python
import functools
import math

import jax
import jax.numpy as jnp
from jax import lax
from jax.experimental import pallas as pl
from jax.experimental.pallas import tpu as pltpu
from jax.sharding import PartitionSpec as P


BLOCK = 32
POWERS = 4
BASIS = 96
WIDE = BLOCK * POWERS

PRECISE = lax.Precision.HIGHEST
OPERATOR_SCALE = 11.0
DEGREE = 6.0
LANES = 128
SUBLANES = 8
F32 = jnp.float32
BF16 = jnp.bfloat16
AXES = ("gx", "gy", "gz")


def lane_of(shape):
    return lax.broadcasted_iota(jnp.int32, shape, 1)


def row_of(shape):
    return lax.broadcasted_iota(jnp.int32, shape, 0)


def kernel_call(body, shapes, scratch=(), in_specs=None, cost=None, limit=24 * 1024 * 1024):
    options = {} if in_specs is None else {"in_specs": in_specs}
    return pl.pallas_call(
        body,
        out_shape=[jax.ShapeDtypeStruct(shape, F32) for shape in shapes],
        scratch_shapes=list(scratch),
        compiler_params=pltpu.CompilerParams(vmem_limit_bytes=limit),
        cost_estimate=cost,
        **options,
    )


def even_on(axis):
    return lax.axis_index(axis) % 2 == 0


def last_on(axis):
    return lax.axis_index(axis) == lax.axis_size(axis) - 1


def sides(axis, first, second):
    even = even_on(axis)
    above = jnp.where(last_on(axis), 0.0, jnp.where(even, first, second))
    below = jnp.where(lax.axis_index(axis) == 0, 0.0, jnp.where(even, second, first))
    return above, below


def pick(even, first, second):
    return jnp.where(even, first, second)


def pack_body(prior_hbm, weights_hbm, field_ref, *refs):
    face_refs, (prior_ref, weights_ref, prior_sem, weights_sem) = refs[:-4], refs[-4:]
    size_x, size_y, width = field_ref.shape
    weights_copy = pltpu.make_async_copy(weights_hbm, weights_ref, weights_sem)
    copies = [pltpu.make_async_copy(prior_hbm.at[i], prior_ref.at[i], prior_sem.at[i]) for i in range(size_x)]
    weights_copy.start()
    for copy in copies:
        copy.start()
    own = width - LANES
    size_z = own // BLOCK
    shape = (size_y, LANES)
    lane = lane_of(shape)
    even = even_on("gz")
    weights_copy.wait()
    for i in range(size_x):
        pieces = [weights_ref[d, i] for d in range(3)]
        pieces.append(jnp.zeros((size_y, LANES - 3 * size_z), F32))
        weights = jnp.concatenate(pieces, axis=1)
        field_ref[i, :, own:] = weights
        for face_ref in face_refs:
            face_ref[i, :, LANES:] = weights
    for i in range(size_x):
        copies[i].wait()
        values = []
        for q in range(own // LANES):
            tiles = [prior_ref[i, :, (3 * q + m) * LANES : (3 * q + m + 1) * LANES] for m in range(3)]
            low, high = pltpu.roll(tiles[0], 64, 1), pltpu.roll(tiles[2], 64, 1)
            value = jnp.where(lane < 64, jnp.where(lane < 32, low, tiles[1]), jnp.where(lane < 96, high, tiles[2]))
            field_ref[i, :, q * LANES : (q + 1) * LANES] = value
            values.append(value)
        faces = [pick(even, values[-1], values[0]), pick(even, values[0], values[-1])]
        for face_ref, face in zip(face_refs, faces):
            face_ref[i, :, :LANES] = face


def widen_body(field_ref, *refs):
    halo_refs, (wide_ref, *face_refs) = refs[:-3], refs[-3:]
    size_x, size_y, width = field_ref.shape
    own = width - LANES
    size_z = own // BLOCK
    lane = lane_of((size_y, LANES))
    upper = (lane % size_z) < size_z // 2
    even_y = even_on("gy")
    zero = jnp.zeros((size_y, LANES), F32)
    for i in range(size_x):
        values = [ref[i, :, :LANES] for ref in halo_refs] + [zero, zero]
        others = [ref[i, :, LANES:] for ref in halo_refs] + [zero, zero]
        above, below = sides("gz", values[0], values[1])
        above_w, below_w = sides("gz", others[0], others[1])
        other = pltpu.roll(jnp.where(upper, above_w, below_w), 3 * size_z, 1)
        weights = jnp.where(lane < 3 * size_z, field_ref[i, :, own:], jnp.where(lane < 6 * size_z, other, zero))
        row = jnp.concatenate([field_ref[i, :, :own], above, below, weights], axis=1)
        wide_ref[i] = row
        low, high = row[:POWERS], row[size_y - POWERS :]
        face_refs[0][i] = pick(even_y, high, low)
        face_refs[1][i] = pick(even_y, low, high)


def lengthen_body(wide_ref, first_ref, second_ref, long_ref, *rest_refs):
    size_x, size_y, width = wide_ref.shape
    even_x = even_on("gx")
    rest = []
    for i in range(size_x):
        wide = wide_ref[i]
        long_ref[i, :size_y] = wide
        halo = jnp.concatenate(sides("gy", first_ref[i], second_ref[i]), axis=0)
        long_ref[i, size_y:] = halo
        side = wide[:, width - 3 * LANES :]
        pieces = [side[row : row + SUBLANES] for row in range(0, size_y, SUBLANES)]
        rest.append(jnp.concatenate(pieces + [halo], axis=1))
    for at in range(POWERS - 1):
        low, high = rest[at], rest[size_x - POWERS + 1 + at]
        rest_refs[0][at] = pick(even_x, high, low)
        rest_refs[1][at] = pick(even_x, low, high)


def contract(left, right):
    return lax.dot_general(
        left, right, (((0,), (0,)), ((), ())), precision=PRECISE, preferred_element_type=F32
    )


def prior_body(prior_ref, q_ref, inner_ref):
    size_x, size_y, width = prior_ref.shape
    size_z = width // BASIS
    lane = lane_of((size_y, LANES))
    for i in range(size_x):
        for q in range(width // (3 * LANES)):
            prior = [prior_ref[i, :, (3 * q + m) * LANES : (3 * q + m + 1) * LANES] for m in range(3)]
            rows = [
                prior[0],
                jnp.where(lane < 32, pltpu.roll(prior[0], 32, 1), pltpu.roll(prior[1], 32, 1)),
                jnp.where(lane < 64, pltpu.roll(prior[1], 64, 1), pltpu.roll(prior[2], 64, 1)),
                pltpu.roll(prior[2], 96, 1),
            ]
            for r in range(4):
                at = (i * size_z + 4 * q + r) * size_y
                q_ref[at : at + size_y] = jnp.where(lane < BASIS, rows[r], 0.0)
    rows = q_ref[...]
    inner_ref[...] = contract(rows, rows)[:BASIS]


def exact_dot(values, selector):
    high = values.astype(BF16)
    rest = values - high.astype(F32)
    middle = rest.astype(BF16)
    low = (rest - middle.astype(F32)).astype(BF16)
    dot = functools.partial(jnp.dot, preferred_element_type=F32)
    return dot(high, selector) + dot(middle, selector) + dot(low, selector)


def columns_body(size_z, own_ref, near_ref, far_ref, near_rest_ref, far_rest_ref, q_ref, inner_ref, s_ref, keep_ref, give_ref, joined, coupling, diagonal, levels, sums):
    size_x, rows, width = own_ref.shape
    size_y = rows - 2 * POWERS
    field = width - LANES
    own = size_z * BLOCK
    planes = size_x + 2 * POWERS
    joined[:size_x] = own_ref[...]
    for at in range(POWERS):
        high = near_ref.shape[0] - POWERS + at
        above, _ = sides("gx", near_ref[at], far_ref[at])
        _, below = sides("gx", near_ref[high], far_ref[high])
        for p, value in ((size_x + at, above), (size_x + POWERS + at, below)):
            joined[p, :size_y, :own] = value[:, :own]
            joined[p, :size_y, field:] = value[:, own:]
    zero = jnp.zeros((size_y, 2 * LANES), F32)
    for p in (size_x + POWERS - 1, size_x + POWERS):
        joined[p, :size_y, own:field] = zero
        joined[p, size_y:] = jnp.zeros((2 * POWERS, width), F32)
    for at in range(POWERS - 1):
        above, below = sides("gx", near_rest_ref[at], far_rest_ref[at])
        for p, value in ((size_x + at, above), (size_x + POWERS + 1 + at, below)):
            for part in range(size_y // SUBLANES):
                lanes = slice(3 * part * LANES, 3 * (part + 1) * LANES)
                joined[p, part * SUBLANES : (part + 1) * SUBLANES, own:] = value[:, lanes]
            joined[p, size_y:] = value[:, 3 * (size_y // SUBLANES) * LANES :]

    weights = joined[:, :, field:].reshape(-1, LANES)
    source = row_of((LANES, field))
    position = lane_of((LANES, field)) // BLOCK
    place = jnp.where(
        position < size_z,
        position,
        jnp.where(position < size_z + POWERS, position + 2 * size_z, position + 3 * size_z - 2 * POWERS),
    )
    unit = 1.0 / math.sqrt(DEGREE)
    for d in range(3):
        selector = (source == place + d * size_z).astype(F32).astype(BF16)
        spread = exact_dot(weights, selector) * unit
        coupling[d] = spread.reshape(planes, rows, field)
    row_last = (row_of((rows, field)) == size_y - 1) & last_on("gy")
    lane_last = (lane_of((rows, field)) // BLOCK == size_z - 1) & last_on("gz")

    near = lambda layers: [p for p in range(planes) if p < size_x + layers or p >= planes - layers]
    for p in near(POWERS - 1):
        x, y, z = (coupling[d, p] for d in range(3))
        x_low = coupling[0, (p - 1) % planes]
        diagonal[p] = x + x_low + (y + pltpu.roll(y, 1, 0)) + (z + pltpu.roll(z, BLOCK, 1)) - math.sqrt(DEGREE)
    for p in near(POWERS - 1):
        coupling[1, p] = jnp.where(row_last, 0.0, coupling[1, p])
        coupling[2, p] = jnp.where(lane_last, 0.0, coupling[2, p])
    coupling[0, size_x - 1] = jnp.where(last_on("gx"), 0.0, coupling[0, size_x - 1])

    def level(k, p):
        return joined[p, :, :field] if k == 0 else levels[k - 1, p]

    for k in range(1, POWERS + 1):
        for p in near(POWERS - k):
            value = level(k - 1, p)
            up, down = (p + 1) % planes, (p - 1) % planes
            x, y, z = (coupling[d, p] for d in range(3))
            total = diagonal[p] * value - x * level(k - 1, up) - coupling[0, down] * level(k - 1, down)
            total = total - y * pltpu.roll(value, rows - 1, 0) - pltpu.roll(y * value, 1, 0)
            total = total - z * pltpu.roll(value, field - BLOCK, 1) - pltpu.roll(z * value, BLOCK, 1)
            if k > 1:
                total = total - level(k - 2, p)
            if k == POWERS:
                levels[k - 1, p, :size_y, :own] = total[:size_y, :own]
            else:
                levels[k - 1, p] = total

    lane = lane_of((size_y, LANES))
    block = lane // BLOCK
    for i in range(size_x):
        for q in range(own // LANES):
            tiles = [levels[m, i, :size_y, q * LANES : (q + 1) * LANES] for m in range(POWERS)]
            for r in range(4):
                moved = [pltpu.roll(tiles[m], (32 * (m - r)) % LANES, 1) if m != r else tiles[m] for m in range(POWERS)]
                at = (i * size_z + 4 * q + r) * size_y
                s_ref[at : at + size_y] = by_block(block, moved)

    columns = s_ref[...]
    sums[:BASIS] = contract(q_ref[...], columns)[:BASIS]
    last = contract(columns[:, WIDE - BLOCK :], columns)
    inner = inner_ref[...]
    block = lane_of((BLOCK, LANES)) // BLOCK
    turned = pltpu.roll(last, 96, 1)
    sums[BASIS : BASIS + 32] = jnp.where(block < 3, inner[:32], turned)
    sums[BASIS + 32 : BASIS + 64] = by_block(block, [turned, inner[32:64], inner[32:64], pltpu.roll(last, 32, 1)])
    block = block[:16]
    sums[BASIS + 64 :] = by_block(
        block,
        [pltpu.roll(inner[64:80], 64, 1), pltpu.roll(inner[80:96], 96, 1), pltpu.roll(last[:16], 96, 1), last[16:]],
    )
    half = sums.shape[0] // 2
    even = even_on("gx")
    keep_ref[...] = pick(even, sums[:half], sums[half:])
    give_ref[...] = pick(even, sums[half:], sums[:half])


def by_block(block, values):
    return jnp.where(
        block < 2, jnp.where(block < 1, values[0], values[1]), jnp.where(block < 3, values[2], values[3])
    )


def unpack(sums):
    cross = sums[:BASIS]
    top, middle, tail = sums[BASIS : BASIS + 32], sums[BASIS + 32 : BASIS + 64], sums[BASIS + 64 : BASIS + 80]
    block = lane_of((BLOCK, LANES)) // BLOCK
    corner = jnp.concatenate([pltpu.roll(tail, 64, 1), pltpu.roll(tail, 32, 1)], axis=0)
    moment = jnp.concatenate([tail, pltpu.roll(tail, 96, 1)], axis=0)
    last = jnp.concatenate([pltpu.roll(tail, 32, 1), tail], axis=0)
    upper = jnp.concatenate([top, middle, corner, jnp.zeros((BLOCK, LANES), F32)], axis=0)
    row, lane = row_of((BASIS, LANES)) // BLOCK, lane_of((BASIS, LANES)) // BLOCK
    inner = jnp.where(row <= lane, upper[:BASIS], jnp.transpose(upper)[:BASIS])
    inner = jnp.where(lane < BASIS // BLOCK, inner, 0.0)
    moments = cross[BASIS - BLOCK :]
    half = pltpu.roll(moments, 64, 1)
    first = jnp.where(block == 0, moment, pltpu.roll(moments, 32, 1)) + pltpu.roll(moments, 96, 1)
    first = jnp.where(block == 3, top, first)
    second = jnp.where(block == 2, half + pltpu.roll(top, 96, 1), pltpu.roll(moment, 32, 1) + moments + half)
    second = jnp.where(block == 3, pltpu.roll(middle, 96, 1), second)
    third = jnp.where(block == 3, middle, corner + pltpu.roll(middle, 64, 1))
    return inner, cross, jnp.concatenate([first, second, third, last], axis=0)


def split_rows(values):
    high = values.astype(BF16).astype(F32)
    rest = values - high
    middle = rest.astype(BF16).astype(F32)
    low = rest - middle
    left = jnp.concatenate([high, high, middle, high, low, middle], axis=0).astype(BF16)
    right = jnp.concatenate([high, middle, high, low, high, middle], axis=0).astype(BF16)
    return left, right


def factor_panel(left, right, column):
    size, count = left.shape
    entry = lambda i, j: jnp.broadcast_to(left[i : i + 1, column + j : column + j + 1], (size, count))
    a = {(i, j): entry(i, j) for i in range(size) for j in range(i, size)}
    row_a = [jnp.broadcast_to(left[i : i + 1, :], (size, count)) for i in range(size)]
    row_b = [jnp.broadcast_to(right[i : i + 1, :], (size, count)) for i in range(size)]
    for k in range(size):
        inverse = lax.rsqrt(a[k, k])
        row_a[k] = row_a[k] * inverse
        row_b[k] = row_b[k] * inverse
        scaled = {j: a[k, j] * inverse for j in range(k + 1, size)}
        for i in range(k + 1, size):
            for j in range(i, size):
                a[i, j] = a[i, j] - scaled[i] * scaled[j]
            row_a[i] = row_a[i] - scaled[i] * row_a[k]
            row_b[i] = row_b[i] - scaled[i] * row_b[k]
    sub = row_of((size, count))
    out_a, out_b = row_a[0], row_b[0]
    for i in range(1, size):
        out_a, out_b = jnp.where(sub == i, row_a[i], out_a), jnp.where(sub == i, row_b[i], out_b)
    return out_a, out_b


def factor(joined, upper, inverse):
    count = upper.shape[0]
    for start in range(0, count, SUBLANES):
        stop = start + SUBLANES
        out_a, out_b = factor_panel(joined[start:stop, :count], joined[start:stop, count:], start)
        shape = (SUBLANES, count)
        out_a = jnp.where(lane_of(shape) >= row_of(shape) + start, out_a, 0.0)
        upper[start:stop] = out_a
        inverse[start:stop] = out_b
        if stop < count:
            left, right = split_rows(jnp.concatenate([out_a, out_b], axis=1))
            update = lax.dot_general(
                left[:, :count], right, (((0,), (0,)), ((), ())), preferred_element_type=F32
            )
            joined[stop:] = joined[stop:] - update[stop:]


def basis_change(centre, width):
    def apply_a(c):
        up = [0.0] + [width * v for v in c[:-1]]
        down = [width * v for v in c[1:]] + [0.0]
        return [centre * v + u + d for v, u, d in zip(c, up, down)]

    def apply_x(c):
        out = [0.0] * len(c)
        out[1] = out[1] + c[0]
        for k in range(1, len(c)):
            if k + 1 < len(c):
                out[k + 1] = out[k + 1] + 0.5 * c[k]
            out[k - 1] = out[k - 1] + 0.5 * c[k]
        return [(o - centre * v) * (1.0 / width) for o, v in zip(out, c)]

    one = centre * 0.0 + 1.0
    t = [[one] + [0.0] * POWERS]
    s = [[one] + [0.0] * POWERS]
    t.append(apply_a(t[0]))
    s.append(apply_x(s[0]))
    for _ in range(1, POWERS):
        t.append([2.0 * v - w for v, w in zip(apply_a(t[-1]), t[-2])])
        s.append([v - w for v, w in zip(apply_x(s[-1]), s[-2])])
    return t, s


def per_block(values):
    block = lane_of((SUBLANES, WIDE)) // BLOCK
    out = jnp.zeros((SUBLANES, WIDE), F32)
    for k, value in enumerate(values):
        out = jnp.where(block == k, value, out)
    return out[:1]


def finish_body(scale, shift_ref, q_ref, s_ref, mine_ref, other_ref, basis_ref, projection_ref, triangle_ref, joined, upper, inverse):
    size_x, size_y, width = basis_ref.shape
    size_z = width // WIDE
    even = even_on("gx")
    mine, other = mine_ref[...] * scale, other_ref[...] * scale
    sums = jnp.concatenate([pick(even, mine, other), pick(even, other, mine)], axis=0)
    dot = functools.partial(jnp.dot, precision=PRECISE, preferred_element_type=F32)

    centre, spread = shift_ref[0] * (1.0 / OPERATOR_SCALE) - 1.0, math.sqrt(DEGREE) / OPERATOR_SCALE
    t, s = basis_change(centre, spread)
    constant = per_block([t[k][0] for k in range(1, POWERS + 1)])
    removed = per_block([-s[k][0] for k in range(1, POWERS + 1)])
    mixes = [
        per_block([t[k][k - m] if k > m else 0.0 for k in range(1, POWERS + 1)]) for m in range(POWERS)
    ]

    def to_powers(values):
        total = values * mixes[0]
        for m in range(1, POWERS):
            total = total + pltpu.roll(values, m * BLOCK, 1) * mixes[m]
        return total

    inner, cross, square = unpack(sums)
    shape = inner.shape
    row, lane = row_of(shape), lane_of(shape)
    block = lane // BLOCK
    defect = jnp.where(row == lane, 1.0, 0.0) - inner
    first = (BASIS - BLOCK) // BLOCK
    copies = [pltpu.roll(defect, ((k - first) * BLOCK) % WIDE, 1) if k != first else defect for k in range(POWERS)]
    start = jnp.where(block < 2, jnp.where(block < 1, copies[0], copies[1]), jnp.where(block < 3, copies[2], copies[3]))
    start_defect = dot(defect[:, :BASIS], start)
    both = cross + dot(defect[:, :BASIS], cross)
    moved = both - start_defect * removed
    start_unit = jnp.where(row - (BASIS - BLOCK) == lane - block * BLOCK, 1.0, 0.0)
    projection_ref[...] = to_powers(both) + (start_unit - start_defect) * constant
    left = cross - dot(inner[:, :BASIS], moved)
    product = contract(jnp.concatenate([cross, moved], axis=0), jnp.concatenate([moved, left], axis=0))
    joined[:, :WIDE] = square - product
    shape = (WIDE, WIDE)
    joined[:, WIDE:] = jnp.where(row_of(shape) == lane_of(shape), 1.0, 0.0)
    padded = jnp.concatenate([moved, jnp.zeros((WIDE - BASIS, WIDE), F32)], axis=0)
    twice = s_ref[...] - dot(q_ref[...], padded)
    factor(joined, upper, inverse)
    triangle_ref[...] = to_powers(upper[...])
    new_basis = lax.dot_general(
        twice, inverse[...], (((1,), (1,)), ((), ())), precision=PRECISE, preferred_element_type=F32
    )
    for i in range(size_x):
        for k in range(size_z):
            at = (i * size_z + k) * size_y
            basis_ref[i, :, k * WIDE : (k + 1) * WIDE] = new_basis[at : at + size_y]


def swap(values, axis, step):
    count = lax.axis_size(axis)
    return lax.ppermute(values, axis, [(i, i ^ step) for i in range(count)])


def exchange(first, second, axis, helper):
    count, others = lax.axis_size(axis), lax.axis_size(helper)
    near = [(i, i + 1) for i in range(0, count - 1, 2)]
    far = [(i, i + 1) for i in range(1, count - 1, 2)]
    axes = tuple(name for name in AXES if name in (axis, helper))
    place = lambda at: at[0] * others + at[1] if axes[0] == axis else at[1] * count + at[0]
    got = []
    for value, pairs in ((first, near), (second, far)):
        if not pairs:
            continue
        links = [((i, k), (j, k)) for pair in pairs for i, j in (pair, pair[::-1]) for k in range(others)]
        if others % 2 == 0:
            alone = [i for i in range(count) if not any(i in pair for pair in pairs)]
            links += [((i, k), (i, k ^ 1)) for i in alone for k in range(others)]
        got.append(lax.ppermute(value, axes, [(place(source), place(target)) for source, target in links]))
    return got


def filled(halos, like):
    return halos + [jnp.zeros_like(like)] * (2 - len(halos))


def doublings(axis):
    count = lax.axis_size(axis)
    return [1 << k for k in range(count.bit_length() - 1)]


def cycle(prior_basis, edge_weights, spectral_shift):
    size_x, size_y, _ = prior_basis.shape
    size_z = prior_basis.shape[2] // BASIS
    own = size_z * BLOCK
    cell_local = size_x * size_y * size_z
    cell_count = cell_local
    for axis in AXES:
        cell_count = cell_count * lax.axis_size(axis)

    hbm = pl.BlockSpec(memory_space=pltpu.HBM)
    faces = min(lax.axis_size("gz") - 1, 2)
    field, *faces = kernel_call(
        pack_body,
        [(size_x, size_y, own + LANES)] + [(size_x, size_y, 2 * LANES)] * faces,
        [
            pltpu.VMEM(prior_basis.shape, F32),
            pltpu.VMEM(edge_weights.shape, F32),
            pltpu.SemaphoreType.DMA((size_x,)),
            pltpu.SemaphoreType.DMA(()),
        ],
        [hbm, hbm],
    )(*(pltpu.with_memory_space_constraint(array, pltpu.HBM) for array in (prior_basis, edge_weights)))
    halos = exchange(faces[0], faces[-1], "gz", "gx") if faces else []
    planes_x = filled(exchange(field, field, "gx", "gz"), field)
    degree_shift = spectral_shift + DEGREE
    prior_rows, inner = kernel_call(
        prior_body,
        [(cell_local, LANES), (BASIS, LANES)],
        cost=pl.CostEstimate(flops=6 * 2 * cell_local * LANES * LANES, bytes_accessed=4 * prior_basis.size, transcendentals=0),
    )(prior_basis)
    width = own + 3 * LANES
    wide, first, second = kernel_call(
        widen_body, [(size_x, size_y, width)] + [(size_x, POWERS, width)] * 2
    )(field, *halos)
    halos = filled(exchange(first, second, "gy", "gx"), first)
    rest = (POWERS - 1, SUBLANES, 3 * LANES * (size_y // SUBLANES) + width)
    long, first, second = kernel_call(lengthen_body, [(size_x, size_y + 2 * POWERS, width), rest, rest])(wide, *halos)
    rests = filled(exchange(first, second, "gx", "gz"), first)

    rows, planes, lanes = size_y + 2 * POWERS, size_x + 2 * POWERS, own + 2 * LANES
    sum_rows = BASIS + 80
    half = (sum_rows // 2, WIDE)
    columns, keep, give = kernel_call(
        functools.partial(columns_body, size_z),
        [(cell_local, WIDE), half, half],
        [
            pltpu.VMEM((planes, rows, width), F32),
            pltpu.VMEM((3, planes, rows, lanes), F32),
            pltpu.VMEM((planes, rows, lanes), F32),
            pltpu.VMEM((POWERS, planes, rows, lanes), F32),
            pltpu.VMEM((sum_rows, WIDE), F32),
        ],
    )(long, *planes_x, *rests, prior_rows, inner)

    total = keep + swap(give, "gx", 1)
    for axis in ("gx", "gz", "gy"):
        for step in doublings(axis):
            if (axis, step) != ("gx", 1):
                total = total + swap(total, axis, step)
    other = swap(total, "gx", 1)

    new_basis, projection, triangle = pl.pallas_call(
        functools.partial(finish_body, 1.0 / cell_count),
        in_specs=[pl.BlockSpec(memory_space=pltpu.SMEM)] + [pl.BlockSpec(memory_space=pltpu.VMEM)] * 4,
        out_shape=[
            jax.ShapeDtypeStruct((size_x, size_y, size_z * WIDE), F32),
            jax.ShapeDtypeStruct((BASIS, WIDE), F32),
            jax.ShapeDtypeStruct((WIDE, WIDE), F32),
        ],
        scratch_shapes=[
            pltpu.VMEM((WIDE, 2 * WIDE), F32),
            pltpu.VMEM((WIDE, WIDE), F32),
            pltpu.VMEM((WIDE, WIDE), F32),
        ],
        compiler_params=pltpu.CompilerParams(vmem_limit_bytes=24 * 1024 * 1024),
    )(degree_shift, prior_rows, columns, total, other)
    return new_basis, projection, triangle


def solution(mesh):
    return jax.shard_map(
        cycle,
        mesh=mesh,
        in_specs=(P("gx", "gy", "gz"), P(None, "gx", "gy", "gz"), P()),
        out_specs=(P("gx", "gy", "gz"), P(), P()),
        check_vma=False,
    )
```

```python
import functools
import math

import jax
import jax.numpy as jnp
from jax import lax
from jax.experimental import pallas as pl
from jax.experimental.pallas import tpu as pltpu
from jax.sharding import PartitionSpec as P


BLOCK = 32
POWERS = 4
BASIS = 96
WIDE = BLOCK * POWERS

PRECISE = lax.Precision.HIGHEST
OPERATOR_SCALE = 11.0
DEGREE = 6.0
LANES = 128
SUBLANES = 8
F32 = jnp.float32
BF16 = jnp.bfloat16
AXES = ("gx", "gy", "gz")


def lane_of(shape):
    return lax.broadcasted_iota(jnp.int32, shape, 1)


def row_of(shape):
    return lax.broadcasted_iota(jnp.int32, shape, 0)


def kernel_call(body, shapes, scratch=(), in_specs=None, cost=None, limit=24 * 1024 * 1024):
    options = {} if in_specs is None else {"in_specs": in_specs}
    return pl.pallas_call(
        body,
        out_shape=[shape if isinstance(shape, jax.ShapeDtypeStruct) else jax.ShapeDtypeStruct(shape, F32) for shape in shapes],
        scratch_shapes=list(scratch),
        compiler_params=pltpu.CompilerParams(vmem_limit_bytes=limit),
        cost_estimate=cost,
        **options,
    )


def even_on(axis):
    return lax.axis_index(axis) % 2 == 0


def last_on(axis):
    return lax.axis_index(axis) == lax.axis_size(axis) - 1


def sides(axis, first, second):
    even = even_on(axis)
    above = jnp.where(last_on(axis), 0.0, jnp.where(even, first, second))
    below = jnp.where(lax.axis_index(axis) == 0, 0.0, jnp.where(even, second, first))
    return above, below


def pick(even, first, second):
    return jnp.where(even, first, second)


def pack_body(prior_hbm, weights_hbm, field_ref, *refs):
    face_refs, (prior_ref, weights_ref, prior_sem, weights_sem) = refs[:-4], refs[-4:]
    size_x, size_y, width = field_ref.shape
    weights_copy = pltpu.make_async_copy(weights_hbm, weights_ref, weights_sem)
    copies = [pltpu.make_async_copy(prior_hbm.at[i], prior_ref.at[i], prior_sem.at[i]) for i in range(size_x)]
    weights_copy.start()
    for copy in copies:
        copy.start()
    own = width - LANES
    size_z = own // BLOCK
    shape = (size_y, LANES)
    lane = lane_of(shape)
    even = even_on("gz")
    weights_copy.wait()
    for i in range(size_x):
        pieces = [weights_ref[d, i] for d in range(3)]
        pieces.append(jnp.zeros((size_y, LANES - 3 * size_z), F32))
        weights = jnp.concatenate(pieces, axis=1)
        field_ref[i, :, own:] = weights
        for face_ref in face_refs:
            face_ref[i, :, LANES:] = weights
    for i in range(size_x):
        copies[i].wait()
        values = []
        for q in range(own // LANES):
            tiles = [prior_ref[i, :, (3 * q + m) * LANES : (3 * q + m + 1) * LANES] for m in range(3)]
            low, high = pltpu.roll(tiles[0], 64, 1), pltpu.roll(tiles[2], 64, 1)
            value = jnp.where(lane < 64, jnp.where(lane < 32, low, tiles[1]), jnp.where(lane < 96, high, tiles[2]))
            field_ref[i, :, q * LANES : (q + 1) * LANES] = value
            values.append(value)
        faces = [pick(even, values[-1], values[0]), pick(even, values[0], values[-1])]
        for face_ref, face in zip(face_refs, faces):
            face_ref[i, :, :LANES] = face


def nearest(planes, refs):
    even = even_on("gx")
    for at in range(POWERS - 1):
        low, high = planes[at], planes[len(planes) - POWERS + 1 + at]
        refs[0][at] = pick(even, high, low)
        refs[1][at] = pick(even, low, high)


def widen_body(field_ref, *refs):
    halo_refs, (wide_ref, *face_refs) = refs[:-5], refs[-5:]
    size_x, size_y, width = field_ref.shape
    own = width - LANES
    size_z = own // BLOCK
    lane = lane_of((size_y, LANES))
    upper = (lane % size_z) < size_z // 2
    even_y = even_on("gy")
    zero = jnp.zeros((size_y, LANES), F32)
    side = []
    for i in range(size_x):
        values = [ref[i, :, :LANES] for ref in halo_refs] + [zero, zero]
        others = [ref[i, :, LANES:] for ref in halo_refs] + [zero, zero]
        above, below = sides("gz", values[0], values[1])
        above_w, below_w = sides("gz", others[0], others[1])
        other = pltpu.roll(jnp.where(upper, above_w, below_w), 3 * size_z, 1)
        weights = jnp.where(lane < 3 * size_z, field_ref[i, :, own:], jnp.where(lane < 6 * size_z, other, zero))
        row = jnp.concatenate([field_ref[i, :, :own], above, below, weights], axis=1)
        wide_ref[i] = row
        low, high = row[:POWERS], row[size_y - POWERS :]
        face_refs[0][i] = pick(even_y, high, low)
        face_refs[1][i] = pick(even_y, low, high)
        side.append(row[:, own:])
    nearest(side, face_refs[2:])


def lengthen_body(wide_ref, first_ref, second_ref, long_ref, *rest_refs):
    size_x, size_y, _ = wide_ref.shape
    rest = []
    for i in range(size_x):
        long_ref[i, :size_y] = wide_ref[i]
        halo = jnp.concatenate(sides("gy", first_ref[i], second_ref[i]), axis=0)
        long_ref[i, size_y:] = halo
        rest.append(halo)
    nearest(rest, rest_refs)


def contract(left, right):
    return lax.dot_general(
        left, right, (((0,), (0,)), ((), ())), precision=PRECISE, preferred_element_type=F32
    )


def prior_body(prior_ref, q_ref, parts_ref, inner_ref):
    size_x, size_y, width = prior_ref.shape
    size_z = width // BASIS
    lane = lane_of((size_y, LANES))
    for i in range(size_x):
        for q in range(width // (3 * LANES)):
            prior = [prior_ref[i, :, (3 * q + m) * LANES : (3 * q + m + 1) * LANES] for m in range(3)]
            rows = [
                prior[0],
                jnp.where(lane < 32, pltpu.roll(prior[0], 32, 1), pltpu.roll(prior[1], 32, 1)),
                jnp.where(lane < 64, pltpu.roll(prior[1], 64, 1), pltpu.roll(prior[2], 64, 1)),
                pltpu.roll(prior[2], 96, 1),
            ]
            for r in range(4):
                at = (i * size_z + 4 * q + r) * size_y
                q_ref[at : at + size_y] = jnp.where(lane < BASIS, rows[r], 0.0)
    rows = q_ref[...]
    inner_ref[...] = contract(rows, rows)[:BASIS]
    parts_ref[:, :LANES], parts_ref[:, LANES:] = halves(rows)


def halves(values):
    high = values.astype(BF16)
    return high, (values - high.astype(F32)).astype(BF16)


def wide_dot(left_parts, right):
    high, low = halves(right)
    stacked = jnp.concatenate(
        [jnp.concatenate([high, low], axis=1), jnp.concatenate([high, jnp.zeros_like(low)], axis=1)], axis=0
    )
    both = jnp.dot(left_parts, stacked, preferred_element_type=F32)
    count = right.shape[1]
    return both[:, :count] + both[:, count:]


def columns_body(size_z, own_ref, near_ref, far_ref, near_side_ref, far_side_ref, near_rest_ref, far_rest_ref, q_ref, inner_ref, s_ref, keep_ref, give_ref, joined, coupling, diagonal, levels, sums, q_parts, s_parts):
    size_x, rows, width = own_ref.shape
    size_y = rows - 2 * POWERS
    field = width - LANES
    own = size_z * BLOCK
    planes = size_x + 2 * POWERS
    joined[:size_x] = own_ref[...]
    for at in range(POWERS):
        high = near_ref.shape[0] - POWERS + at
        above, _ = sides("gx", near_ref[at], far_ref[at])
        _, below = sides("gx", near_ref[high], far_ref[high])
        for p, value in ((size_x + at, above), (size_x + POWERS + at, below)):
            joined[p, :size_y, :own] = value[:, :own]
            joined[p, :size_y, field:] = value[:, own:]
    zero = jnp.zeros((size_y, 2 * LANES), F32)
    for p in (size_x + POWERS - 1, size_x + POWERS):
        joined[p, :size_y, own:field] = zero
        joined[p, size_y:] = jnp.zeros((2 * POWERS, width), F32)
    for at in range(POWERS - 1):
        halo = sides("gx", near_rest_ref[at], far_rest_ref[at])
        side = sides("gx", near_side_ref[at], far_side_ref[at])
        for up in range(2):
            p = size_x + at + up * (POWERS + 1)
            joined[p, :size_y, own:] = side[up]
            joined[p, size_y:] = halo[up]

    weights = joined[:, :, field:].reshape(-1, LANES)
    weights = jnp.concatenate(halves(weights * (1.0 / math.sqrt(DEGREE))), axis=1)
    source = row_of((2 * LANES, field))
    position = lane_of((2 * LANES, field)) // BLOCK
    place = jnp.where(
        position < size_z,
        position,
        jnp.where(position < size_z + POWERS, position + 2 * size_z, position + 3 * size_z - 2 * POWERS),
    )
    for d in range(3):
        selector = jnp.where(source % LANES == place + d * size_z, 1.0, 0.0).astype(BF16)
        spread = jnp.dot(weights, selector, preferred_element_type=F32)
        coupling[d] = spread.reshape(planes, rows, field)
    row_last = (row_of((rows, field)) == size_y - 1) & last_on("gy")
    lane_last = (lane_of((rows, field)) // BLOCK == size_z - 1) & last_on("gz")

    distance = lambda p: 0 if p < size_x else min(p - size_x + 1, planes - p)
    near = lambda layers: [p for p in range(planes) if p < size_x + layers or p >= planes - layers]
    for p in near(POWERS - 1):
        x, y, z = (coupling[d, p] for d in range(3))
        x_low = coupling[0, (p - 1) % planes]
        diagonal[p] = x + x_low + (y + pltpu.roll(y, 1, 0)) + (z + pltpu.roll(z, BLOCK, 1)) - math.sqrt(DEGREE)
    for p in near(POWERS - 1):
        coupling[1, p] = jnp.where(row_last, 0.0, coupling[1, p])
        coupling[2, p] = jnp.where(lane_last, 0.0, coupling[2, p])
    coupling[0, size_x - 1] = jnp.where(last_on("gx"), 0.0, coupling[0, size_x - 1])

    def level(k, p):
        return joined[p, :, :field] if k == 0 else levels[k - 1, p]

    for k in range(1, POWERS + 1):
        for p in near(POWERS - k):
            value = level(k - 1, p)
            up, down = (p + 1) % planes, (p - 1) % planes
            x, y, z = (coupling[d, p] for d in range(3))
            total = diagonal[p] * value - x * level(k - 1, up) - coupling[0, down] * level(k - 1, down)
            total = total - y * pltpu.roll(value, rows - 1, 0) - pltpu.roll(y * value, 1, 0)
            total = total - z * pltpu.roll(value, field - BLOCK, 1) - pltpu.roll(z * value, BLOCK, 1)
            if k > 1:
                total = total - level(k - 2, p)
            reach = POWERS - k - distance(p)
            if reach == 0:
                levels[k - 1, p, :size_y, :own] = total[:size_y, :own]
            elif reach == 1:
                levels[k - 1, p, :size_y] = total[:size_y]
                levels[k - 1, p, size_y:, :own] = total[size_y:, :own]
            else:
                levels[k - 1, p] = total

    lane = lane_of((size_y, LANES))
    block = lane // BLOCK
    for i in range(size_x):
        for q in range(own // LANES):
            tiles = [levels[m, i, :size_y, q * LANES : (q + 1) * LANES] for m in range(POWERS)]
            for r in range(4):
                moved = [pltpu.roll(tiles[m], (32 * (m - r)) % LANES, 1) if m != r else tiles[m] for m in range(POWERS)]
                at = (i * size_z + 4 * q + r) * size_y
                row = by_block(block, moved)
                s_ref[at : at + size_y] = row
                s_parts[at : at + size_y, :WIDE], s_parts[at : at + size_y, WIDE:] = halves(row)
                row = jnp.where(lane < BASIS, q_ref[at : at + size_y], row)
                q_parts[at : at + size_y, :LANES], q_parts[at : at + size_y, LANES:] = halves(row)

    product = lax.dot_general(
        q_parts[...], s_parts[...], (((0,), (0,)), ((), ())), preferred_element_type=F32
    )
    product = product[:LANES] + product[LANES:]
    product = product[:, :WIDE] + product[:, WIDE:]
    sums[:BASIS] = product[:BASIS]
    last = product[BASIS:]
    inner = inner_ref[...]
    block = lane_of((BLOCK, LANES)) // BLOCK
    turned = pltpu.roll(last, 96, 1)
    sums[BASIS : BASIS + 32] = jnp.where(block < 3, inner[:32], turned)
    sums[BASIS + 32 : BASIS + 64] = by_block(block, [turned, inner[32:64], inner[32:64], pltpu.roll(last, 32, 1)])
    block = block[:16]
    sums[BASIS + 64 :] = by_block(
        block,
        [pltpu.roll(inner[64:80], 64, 1), pltpu.roll(inner[80:96], 96, 1), pltpu.roll(last[:16], 96, 1), last[16:]],
    )
    half = sums.shape[0] // 2
    even = even_on("gx")
    keep_ref[...] = pick(even, sums[:half], sums[half:])
    give_ref[...] = pick(even, sums[half:], sums[:half])


def by_block(block, values):
    return jnp.where(
        block < 2, jnp.where(block < 1, values[0], values[1]), jnp.where(block < 3, values[2], values[3])
    )


def unpack(sums):
    cross = sums[:BASIS]
    top, middle, tail = sums[BASIS : BASIS + 32], sums[BASIS + 32 : BASIS + 64], sums[BASIS + 64 : BASIS + 80]
    block = lane_of((BLOCK, LANES)) // BLOCK
    corner = jnp.concatenate([pltpu.roll(tail, 64, 1), pltpu.roll(tail, 32, 1)], axis=0)
    moment = jnp.concatenate([tail, pltpu.roll(tail, 96, 1)], axis=0)
    last = jnp.concatenate([pltpu.roll(tail, 32, 1), tail], axis=0)
    upper = jnp.concatenate([top, middle, corner, jnp.zeros((BLOCK, LANES), F32)], axis=0)
    row, lane = row_of((BASIS, LANES)) // BLOCK, lane_of((BASIS, LANES)) // BLOCK
    inner = jnp.where(row <= lane, upper[:BASIS], jnp.transpose(upper)[:BASIS])
    inner = jnp.where(lane < BASIS // BLOCK, inner, 0.0)
    moments = cross[BASIS - BLOCK :]
    half = pltpu.roll(moments, 64, 1)
    first = jnp.where(block == 0, moment, pltpu.roll(moments, 32, 1)) + pltpu.roll(moments, 96, 1)
    first = jnp.where(block == 3, top, first)
    second = jnp.where(block == 2, half + pltpu.roll(top, 96, 1), pltpu.roll(moment, 32, 1) + moments + half)
    second = jnp.where(block == 3, pltpu.roll(middle, 96, 1), second)
    third = jnp.where(block == 3, middle, corner + pltpu.roll(middle, 64, 1))
    return inner, cross, jnp.concatenate([first, second, third, last], axis=0)


def split_rows(values):
    high = values.astype(BF16).astype(F32)
    rest = values - high
    middle = rest.astype(BF16).astype(F32)
    low = rest - middle
    left = jnp.concatenate([high, high, middle, high, low, middle], axis=0).astype(BF16)
    right = jnp.concatenate([high, middle, high, low, high, middle], axis=0).astype(BF16)
    return left, right


def factor(joined, upper, inverse):
    count = upper.shape[0]
    shape = (SUBLANES, count)
    sub, lane = row_of(shape), lane_of(shape)
    panel = range(SUBLANES)
    entry = lambda rows, i, j: jnp.broadcast_to(rows[i : i + 1, j : j + 1], shape)
    spread = lambda rows: [jnp.broadcast_to(rows[i : i + 1], shape) for i in panel]

    def entries(rows, start):
        return {(i, j): entry(rows[i], 0, start + j) for i in panel for j in panel if j >= i}

    rows_a = spread(joined[:SUBLANES, :count])
    a = entries(rows_a, 0)
    for start in range(0, count, SUBLANES):
        stop = start + SUBLANES
        following = spread(joined[stop : stop + SUBLANES, :count]) if stop < count else None
        rows_b = spread(joined[start:stop, count:])
        for k in panel:
            scale = lax.rsqrt(a[k, k])
            rows_a[k], rows_b[k] = rows_a[k] * scale, rows_b[k] * scale
            scaled = {j: a[k, j] * scale for j in panel if j > k}
            for i in scaled:
                for j in panel:
                    if j >= i:
                        a[i, j] = a[i, j] - scaled[i] * scaled[j]
                rows_a[i] = rows_a[i] - scaled[i] * rows_a[k]
                rows_b[i] = rows_b[i] - scaled[i] * rows_b[k]
        out_a, out_b = rows_a[0], rows_b[0]
        for i in panel[1:]:
            out_a, out_b = jnp.where(sub == i, rows_a[i], out_a), jnp.where(sub == i, rows_b[i], out_b)
        out_a = jnp.where(lane >= sub + start, out_a, 0.0)
        upper[start:stop], inverse[start:stop] = out_a, out_b
        if stop == count:
            break
        for k in panel:
            for j in panel:
                following[j] = following[j] - entry(rows_a[k], 0, stop + j) * rows_a[k]
        rows_a, a = following, entries(following, stop)
        left, right = split_rows(jnp.concatenate([out_a, out_b], axis=1))
        update = lax.dot_general(left[:, :count], right, (((0,), (0,)), ((), ())), preferred_element_type=F32)
        after = stop + SUBLANES
        joined[stop:after, count:] = joined[stop:after, count:] - update[stop:after, count:]
        if after < count:
            joined[after:] = joined[after:] - update[after:]


def basis_change(centre, width):
    def apply_a(c):
        up = [0.0] + [width * v for v in c[:-1]]
        down = [width * v for v in c[1:]] + [0.0]
        return [centre * v + u + d for v, u, d in zip(c, up, down)]

    def apply_x(c):
        out = [0.0] * len(c)
        out[1] = out[1] + c[0]
        for k in range(1, len(c)):
            if k + 1 < len(c):
                out[k + 1] = out[k + 1] + 0.5 * c[k]
            out[k - 1] = out[k - 1] + 0.5 * c[k]
        return [(o - centre * v) * (1.0 / width) for o, v in zip(out, c)]

    one = centre * 0.0 + 1.0
    t = [[one] + [0.0] * POWERS]
    s = [[one] + [0.0] * POWERS]
    t.append(apply_a(t[0]))
    s.append(apply_x(s[0]))
    for _ in range(1, POWERS):
        t.append([2.0 * v - w for v, w in zip(apply_a(t[-1]), t[-2])])
        s.append([v - w for v, w in zip(apply_x(s[-1]), s[-2])])
    return t, s


def per_block(values):
    block = lane_of((SUBLANES, WIDE)) // BLOCK
    out = jnp.zeros((SUBLANES, WIDE), F32)
    for k, value in enumerate(values):
        out = jnp.where(block == k, value, out)
    return out[:1]


def finish_body(scale, shift_ref, q_ref, s_ref, mine_ref, other_ref, basis_ref, projection_ref, triangle_ref, joined, upper, inverse):
    size_x, size_y, width = basis_ref.shape
    size_z = width // WIDE
    even = even_on("gx")
    mine, other = mine_ref[...] * scale, other_ref[...] * scale
    sums = jnp.concatenate([pick(even, mine, other), pick(even, other, mine)], axis=0)
    dot = functools.partial(jnp.dot, precision=PRECISE, preferred_element_type=F32)

    centre, spread = shift_ref[0] * (1.0 / OPERATOR_SCALE) - 1.0, math.sqrt(DEGREE) / OPERATOR_SCALE
    t, s = basis_change(centre, spread)
    constant = per_block([t[k][0] for k in range(1, POWERS + 1)])
    removed = per_block([-s[k][0] for k in range(1, POWERS + 1)])
    mixes = [
        per_block([t[k][k - m] if k > m else 0.0 for k in range(1, POWERS + 1)]) for m in range(POWERS)
    ]

    def to_powers(values):
        total = values * mixes[0]
        for m in range(1, POWERS):
            total = total + pltpu.roll(values, m * BLOCK, 1) * mixes[m]
        return total

    inner, cross, square = unpack(sums)
    shape = inner.shape
    row, lane = row_of(shape), lane_of(shape)
    block = lane // BLOCK
    defect = jnp.where(row == lane, 1.0, 0.0) - inner
    first = (BASIS - BLOCK) // BLOCK
    copies = [pltpu.roll(defect, ((k - first) * BLOCK) % WIDE, 1) if k != first else defect for k in range(POWERS)]
    start = jnp.where(block < 2, jnp.where(block < 1, copies[0], copies[1]), jnp.where(block < 3, copies[2], copies[3]))
    start_defect = dot(defect[:, :BASIS], start)
    both = cross + dot(defect[:, :BASIS], cross)
    moved = both - start_defect * removed
    start_unit = jnp.where(row - (BASIS - BLOCK) == lane - block * BLOCK, 1.0, 0.0)
    projection_ref[...] = to_powers(both) + (start_unit - start_defect) * constant
    left = cross - dot(inner[:, :BASIS], moved)
    product = contract(jnp.concatenate([cross, moved], axis=0), jnp.concatenate([moved, left], axis=0))
    joined[:, :WIDE] = square - product
    shape = (WIDE, WIDE)
    joined[:, WIDE:] = jnp.where(row_of(shape) == lane_of(shape), 1.0, 0.0)
    padded = jnp.concatenate([moved, jnp.zeros((WIDE - BASIS, WIDE), F32)], axis=0)
    twice = s_ref[...] - wide_dot(q_ref[...], padded)
    twice_parts = jnp.concatenate(halves(twice), axis=1)
    factor(joined, upper, inverse)
    triangle_ref[...] = to_powers(upper[...])
    new_basis = wide_dot(twice_parts, jnp.transpose(inverse[...]))
    for i in range(size_x):
        for k in range(size_z):
            at = (i * size_z + k) * size_y
            basis_ref[i, :, k * WIDE : (k + 1) * WIDE] = new_basis[at : at + size_y]


def swap(values, axis, step):
    count = lax.axis_size(axis)
    return lax.ppermute(values, axis, [(i, i ^ step) for i in range(count)])


def exchange(first, second, axis, helper):
    count, others = lax.axis_size(axis), lax.axis_size(helper)
    near = [(i, i + 1) for i in range(0, count - 1, 2)]
    far = [(i, i + 1) for i in range(1, count - 1, 2)]
    axes = tuple(name for name in AXES if name in (axis, helper))
    place = lambda at: at[0] * others + at[1] if axes[0] == axis else at[1] * count + at[0]
    got = []
    for value, pairs in ((first, near), (second, far)):
        if not pairs:
            continue
        links = [((i, k), (j, k)) for pair in pairs for i, j in (pair, pair[::-1]) for k in range(others)]
        if others % 2 == 0:
            alone = [i for i in range(count) if not any(i in pair for pair in pairs)]
            links += [((i, k), (i, k ^ 1)) for i in alone for k in range(others)]
        got.append(lax.ppermute(value, axes, [(place(source), place(target)) for source, target in links]))
    return got


def filled(halos, like):
    return halos + [jnp.zeros_like(like)] * (2 - len(halos))


def doublings(axis):
    count = lax.axis_size(axis)
    return [1 << k for k in range(count.bit_length() - 1)]


def cycle(prior_basis, edge_weights, spectral_shift):
    size_x, size_y, _ = prior_basis.shape
    size_z = prior_basis.shape[2] // BASIS
    own = size_z * BLOCK
    cell_local = size_x * size_y * size_z
    cell_count = cell_local
    for axis in AXES:
        cell_count = cell_count * lax.axis_size(axis)

    hbm = pl.BlockSpec(memory_space=pltpu.HBM)
    faces = min(lax.axis_size("gz") - 1, 2)
    field, *faces = kernel_call(
        pack_body,
        [(size_x, size_y, own + LANES)] + [(size_x, size_y, 2 * LANES)] * faces,
        [
            pltpu.VMEM(prior_basis.shape, F32),
            pltpu.VMEM(edge_weights.shape, F32),
            pltpu.SemaphoreType.DMA((size_x,)),
            pltpu.SemaphoreType.DMA(()),
        ],
        [hbm, hbm],
    )(*(pltpu.with_memory_space_constraint(array, pltpu.HBM) for array in (prior_basis, edge_weights)))
    halos = exchange(faces[0], faces[-1], "gz", "gx") if faces else []
    planes_x = filled(exchange(field, field, "gx", "gz"), field)
    degree_shift = spectral_shift + DEGREE
    prior_rows, prior_parts, inner = kernel_call(
        prior_body,
        [(cell_local, LANES), jax.ShapeDtypeStruct((cell_local, 2 * LANES), BF16), (BASIS, LANES)],
        cost=pl.CostEstimate(flops=6 * 2 * cell_local * LANES * LANES, bytes_accessed=4 * prior_basis.size, transcendentals=0),
    )(prior_basis)
    width = own + 3 * LANES
    side = (POWERS - 1, size_y, 3 * LANES)
    wide, first, second, *side_faces = kernel_call(
        widen_body, [(size_x, size_y, width)] + [(size_x, POWERS, width)] * 2 + [side] * 2
    )(field, *halos)
    halos = filled(exchange(first, second, "gy", "gx"), first)
    sides_x = filled(exchange(*side_faces, "gx", "gz"), side_faces[0])
    rest = (POWERS - 1, 2 * POWERS, width)
    long, first, second = kernel_call(lengthen_body, [(size_x, size_y + 2 * POWERS, width), rest, rest])(wide, *halos)
    rests = filled(exchange(first, second, "gx", "gz"), first)

    rows, planes, lanes = size_y + 2 * POWERS, size_x + 2 * POWERS, own + 2 * LANES
    sum_rows = BASIS + 80
    half = (sum_rows // 2, WIDE)
    columns, keep, give = kernel_call(
        functools.partial(columns_body, size_z),
        [(cell_local, WIDE), half, half],
        [
            pltpu.VMEM((planes, rows, width), F32),
            pltpu.VMEM((3, planes, rows, lanes), F32),
            pltpu.VMEM((planes, rows, lanes), F32),
            pltpu.VMEM((POWERS, planes, rows, lanes), F32),
            pltpu.VMEM((sum_rows, WIDE), F32),
            pltpu.VMEM((cell_local, 2 * LANES), BF16),
            pltpu.VMEM((cell_local, 2 * WIDE), BF16),
        ],
    )(long, *planes_x, *sides_x, *rests, prior_rows, inner)

    total = keep + swap(give, "gx", 1)
    for axis in ("gx", "gz", "gy"):
        for step in doublings(axis):
            if (axis, step) != ("gx", 1):
                total = total + swap(total, axis, step)
    other = swap(total, "gx", 1)

    new_basis, projection, triangle = pl.pallas_call(
        functools.partial(finish_body, 1.0 / cell_count),
        in_specs=[pl.BlockSpec(memory_space=pltpu.SMEM)] + [pl.BlockSpec(memory_space=pltpu.VMEM)] * 4,
        out_shape=[
            jax.ShapeDtypeStruct((size_x, size_y, size_z * WIDE), F32),
            jax.ShapeDtypeStruct((BASIS, WIDE), F32),
            jax.ShapeDtypeStruct((WIDE, WIDE), F32),
        ],
        scratch_shapes=[
            pltpu.VMEM((WIDE, 2 * WIDE), F32),
            pltpu.VMEM((WIDE, WIDE), F32),
            pltpu.VMEM((WIDE, WIDE), F32),
        ],
        compiler_params=pltpu.CompilerParams(vmem_limit_bytes=24 * 1024 * 1024),
    )(degree_shift, prior_parts, columns, total, other)
    return new_basis, projection, triangle


def solution(mesh):
    return jax.shard_map(
        cycle,
        mesh=mesh,
        in_specs=(P("gx", "gy", "gz"), P(None, "gx", "gy", "gz"), P()),
        out_specs=(P("gx", "gy", "gz"), P(), P()),
        check_vma=False,
    )
```

```python
import functools
import math

import jax
import jax.numpy as jnp
from jax import lax
from jax.experimental import pallas as pl
from jax.experimental.pallas import tpu as pltpu
from jax.sharding import PartitionSpec as P


BLOCK = 32
POWERS = 4
BASIS = 96
WIDE = BLOCK * POWERS

PRECISE = lax.Precision.HIGHEST
OPERATOR_SCALE = 11.0
DEGREE = 6.0
LANES = 128
SUBLANES = 8
F32 = jnp.float32
BF16 = jnp.bfloat16
AXES = ("gx", "gy", "gz")


def lane_of(shape):
    return lax.broadcasted_iota(jnp.int32, shape, 1)


def row_of(shape):
    return lax.broadcasted_iota(jnp.int32, shape, 0)


def kernel_call(body, shapes, scratch=(), in_specs=None, cost=None, limit=24 * 1024 * 1024):
    options = {} if in_specs is None else {"in_specs": in_specs}
    return pl.pallas_call(
        body,
        out_shape=[shape if isinstance(shape, jax.ShapeDtypeStruct) else jax.ShapeDtypeStruct(shape, F32) for shape in shapes],
        scratch_shapes=list(scratch),
        compiler_params=pltpu.CompilerParams(vmem_limit_bytes=limit),
        cost_estimate=cost,
        **options,
    )


def even_on(axis):
    return lax.axis_index(axis) % 2 == 0


def last_on(axis):
    return lax.axis_index(axis) == lax.axis_size(axis) - 1


def sides(axis, first, second):
    even = even_on(axis)
    above = jnp.where(last_on(axis), 0.0, jnp.where(even, first, second))
    below = jnp.where(lax.axis_index(axis) == 0, 0.0, jnp.where(even, second, first))
    return above, below


def bits(axis):
    return range((lax.axis_size(axis) - 1).bit_length())


def owns_first_half():
    ones = sum((lax.axis_index(axis) >> k) & 1 for axis in AXES for k in bits(axis))
    return ones % 2 == 0


def pick(even, first, second):
    return jnp.where(even, first, second)


def pack_body(prior_hbm, weights_hbm, field_ref, *refs):
    face_refs, (prior_ref, weights_ref, prior_sem, weights_sem) = refs[:-4], refs[-4:]
    size_x, size_y, width = field_ref.shape
    weights_copy = pltpu.make_async_copy(weights_hbm, weights_ref, weights_sem)
    copies = [pltpu.make_async_copy(prior_hbm.at[i], prior_ref.at[i], prior_sem.at[i]) for i in range(size_x)]
    weights_copy.start()
    for copy in copies:
        copy.start()
    own = width - LANES
    size_z = own // BLOCK
    shape = (size_y, LANES)
    lane = lane_of(shape)
    even = even_on("gz")
    weights_copy.wait()
    for i in range(size_x):
        pieces = [weights_ref[d, i] for d in range(3)]
        pieces.append(jnp.zeros((size_y, LANES - 3 * size_z), F32))
        weights = jnp.concatenate(pieces, axis=1)
        field_ref[i, :, own:] = weights
        for face_ref in face_refs:
            face_ref[i, :, LANES:] = weights
    for i in range(size_x):
        copies[i].wait()
        values = []
        for q in range(own // LANES):
            tiles = [prior_ref[i, :, (3 * q + m) * LANES : (3 * q + m + 1) * LANES] for m in range(3)]
            low, high = pltpu.roll(tiles[0], 64, 1), pltpu.roll(tiles[2], 64, 1)
            value = jnp.where(lane < 64, jnp.where(lane < 32, low, tiles[1]), jnp.where(lane < 96, high, tiles[2]))
            field_ref[i, :, q * LANES : (q + 1) * LANES] = value
            values.append(value)
        faces = [pick(even, values[-1], values[0]), pick(even, values[0], values[-1])]
        for face_ref, face in zip(face_refs, faces):
            face_ref[i, :, :LANES] = face


def nearest(planes, refs):
    even = even_on("gx")
    for at in range(POWERS - 1):
        low, high = planes[at], planes[len(planes) - POWERS + 1 + at]
        refs[0][at] = pick(even, high, low)
        refs[1][at] = pick(even, low, high)


def widen_body(field_ref, *refs):
    halo_refs, (wide_ref, *face_refs) = refs[:-5], refs[-5:]
    size_x, size_y, width = field_ref.shape
    own = width - LANES
    size_z = own // BLOCK
    lane = lane_of((size_y, LANES))
    upper = (lane % size_z) < size_z // 2
    even_y = even_on("gy")
    zero = jnp.zeros((size_y, LANES), F32)
    side = []
    for i in range(size_x):
        values = [ref[i, :, :LANES] for ref in halo_refs] + [zero, zero]
        others = [ref[i, :, LANES:] for ref in halo_refs] + [zero, zero]
        above, below = sides("gz", values[0], values[1])
        above_w, below_w = sides("gz", others[0], others[1])
        other = pltpu.roll(jnp.where(upper, above_w, below_w), 3 * size_z, 1)
        weights = jnp.where(lane < 3 * size_z, field_ref[i, :, own:], jnp.where(lane < 6 * size_z, other, zero))
        row = jnp.concatenate([field_ref[i, :, :own], above, below, weights], axis=1)
        wide_ref[i] = row
        low, high = row[:POWERS], row[size_y - POWERS :]
        face_refs[0][i] = pick(even_y, high, low)
        face_refs[1][i] = pick(even_y, low, high)
        side.append(row[:, own:])
    nearest(side, face_refs[2:])


def lengthen_body(wide_ref, first_ref, second_ref, long_ref, *rest_refs):
    size_x, size_y, _ = wide_ref.shape
    rest = []
    for i in range(size_x):
        long_ref[i, :size_y] = wide_ref[i]
        halo = jnp.concatenate(sides("gy", first_ref[i], second_ref[i]), axis=0)
        long_ref[i, size_y:] = halo
        rest.append(halo)
    nearest(rest, rest_refs)


def contract(left, right):
    return lax.dot_general(
        left, right, (((0,), (0,)), ((), ())), precision=PRECISE, preferred_element_type=F32
    )


def prior_body(prior_ref, q_ref, parts_ref, inner_ref):
    size_x, size_y, width = prior_ref.shape
    size_z = width // BASIS
    lane = lane_of((size_y, LANES))
    for i in range(size_x):
        for q in range(width // (3 * LANES)):
            prior = [prior_ref[i, :, (3 * q + m) * LANES : (3 * q + m + 1) * LANES] for m in range(3)]
            rows = [
                prior[0],
                jnp.where(lane < 32, pltpu.roll(prior[0], 32, 1), pltpu.roll(prior[1], 32, 1)),
                jnp.where(lane < 64, pltpu.roll(prior[1], 64, 1), pltpu.roll(prior[2], 64, 1)),
                pltpu.roll(prior[2], 96, 1),
            ]
            for r in range(4):
                at = (i * size_z + 4 * q + r) * size_y
                q_ref[at : at + size_y] = jnp.where(lane < BASIS, rows[r], 0.0)
    rows = q_ref[...]
    inner_ref[...] = contract(rows, rows)[:BASIS]
    parts_ref[:, :LANES], parts_ref[:, LANES:] = halves(rows)


def halves(values):
    high = values.astype(BF16)
    return high, (values - high.astype(F32)).astype(BF16)


def stacked(right):
    high, low = halves(right)
    return jnp.concatenate(
        [jnp.concatenate([high, low], axis=1), jnp.concatenate([high, jnp.zeros_like(low)], axis=1)], axis=0
    )


def wide_dot(left_parts, right):
    both = jnp.dot(left_parts, right, preferred_element_type=F32)
    count = right.shape[1] // 2
    return both[:, :count] + both[:, count:]


def contract_parts(left, right):
    product = lax.dot_general(left, right, (((0,), (0,)), ((), ())), preferred_element_type=F32)
    rows, columns = left.shape[1] // 2, right.shape[1] // 2
    product = product[:rows] + product[rows:]
    return product[:, :columns] + product[:, columns:]


def columns_body(size_z, own_ref, near_ref, far_ref, near_side_ref, far_side_ref, near_rest_ref, far_rest_ref, q_ref, inner_ref, s_ref, keep_ref, give_ref, joined, coupling, diagonal, levels, sums, q_parts, s_parts):
    size_x, rows, width = own_ref.shape
    size_y = rows - 2 * POWERS
    field = width - LANES
    own = size_z * BLOCK
    planes = size_x + 2 * POWERS
    joined[:size_x] = own_ref[...]
    for at in range(POWERS):
        high = near_ref.shape[0] - POWERS + at
        above, _ = sides("gx", near_ref[at], far_ref[at])
        _, below = sides("gx", near_ref[high], far_ref[high])
        for p, value in ((size_x + at, above), (size_x + POWERS + at, below)):
            joined[p, :size_y, :own] = value[:, :own]
            joined[p, :size_y, field:] = value[:, own:]
    zero = jnp.zeros((size_y, 2 * LANES), F32)
    for p in (size_x + POWERS - 1, size_x + POWERS):
        joined[p, :size_y, own:field] = zero
        joined[p, size_y:] = jnp.zeros((2 * POWERS, width), F32)
    for at in range(POWERS - 1):
        halo = sides("gx", near_rest_ref[at], far_rest_ref[at])
        side = sides("gx", near_side_ref[at], far_side_ref[at])
        for up in range(2):
            p = size_x + at + up * (POWERS + 1)
            joined[p, :size_y, own:] = side[up]
            joined[p, size_y:] = halo[up]

    weights = joined[:, :, field:].reshape(-1, LANES)
    weights = jnp.concatenate(halves(weights * (1.0 / math.sqrt(DEGREE))), axis=1)
    source = row_of((2 * LANES, field))
    position = lane_of((2 * LANES, field)) // BLOCK
    place = jnp.where(
        position < size_z,
        position,
        jnp.where(position < size_z + POWERS, position + 2 * size_z, position + 3 * size_z - 2 * POWERS),
    )
    for d in range(3):
        selector = jnp.where(source % LANES == place + d * size_z, 1.0, 0.0).astype(BF16)
        spread = jnp.dot(weights, selector, preferred_element_type=F32)
        coupling[d] = spread.reshape(planes, rows, field)
    row_last = (row_of((rows, field)) == size_y - 1) & last_on("gy")
    lane_last = (lane_of((rows, field)) // BLOCK == size_z - 1) & last_on("gz")

    distance = lambda p: 0 if p < size_x else min(p - size_x + 1, planes - p)
    near = lambda layers: [p for p in range(planes) if p < size_x + layers or p >= planes - layers]
    for p in near(POWERS - 1):
        x, y, z = (coupling[d, p] for d in range(3))
        x_low = coupling[0, (p - 1) % planes]
        diagonal[p] = x + x_low + (y + pltpu.roll(y, 1, 0)) + (z + pltpu.roll(z, BLOCK, 1)) - math.sqrt(DEGREE)
    for p in near(POWERS - 1):
        coupling[1, p] = jnp.where(row_last, 0.0, coupling[1, p])
        coupling[2, p] = jnp.where(lane_last, 0.0, coupling[2, p])
    coupling[0, size_x - 1] = jnp.where(last_on("gx"), 0.0, coupling[0, size_x - 1])

    def level(k, p):
        return joined[p, :, :field] if k == 0 else levels[k - 1, p]

    for k in range(1, POWERS + 1):
        for p in near(POWERS - k):
            value = level(k - 1, p)
            up, down = (p + 1) % planes, (p - 1) % planes
            x, y, z = (coupling[d, p] for d in range(3))
            total = diagonal[p] * value - x * level(k - 1, up) - coupling[0, down] * level(k - 1, down)
            total = total - y * pltpu.roll(value, rows - 1, 0) - pltpu.roll(y * value, 1, 0)
            total = total - z * pltpu.roll(value, field - BLOCK, 1) - pltpu.roll(z * value, BLOCK, 1)
            if k > 1:
                total = total - level(k - 2, p)
            reach = POWERS - k - distance(p)
            if reach == 0:
                levels[k - 1, p, :size_y, :own] = total[:size_y, :own]
            elif reach == 1:
                levels[k - 1, p, :size_y] = total[:size_y]
                levels[k - 1, p, size_y:, :own] = total[size_y:, :own]
            else:
                levels[k - 1, p] = total

    lane = lane_of((size_y, LANES))
    block = lane // BLOCK
    for i in range(size_x):
        for q in range(own // LANES):
            tiles = [levels[m, i, :size_y, q * LANES : (q + 1) * LANES] for m in range(POWERS)]
            for r in range(4):
                moved = [pltpu.roll(tiles[m], (32 * (m - r)) % LANES, 1) if m != r else tiles[m] for m in range(POWERS)]
                at = (i * size_z + 4 * q + r) * size_y
                row = by_block(block, moved)
                s_ref[at : at + size_y] = row
                s_parts[at : at + size_y, :WIDE], s_parts[at : at + size_y, WIDE:] = halves(row)
                row = jnp.where(lane < BASIS, q_ref[at : at + size_y], row)
                q_parts[at : at + size_y, :LANES], q_parts[at : at + size_y, LANES:] = halves(row)

    product = contract_parts(q_parts[...], s_parts[...])
    sums[:BASIS] = product[:BASIS]
    last = product[BASIS:]
    inner = inner_ref[...]
    block = lane_of((BLOCK, LANES)) // BLOCK
    turned = pltpu.roll(last, 96, 1)
    sums[BASIS : BASIS + 32] = jnp.where(block < 3, inner[:32], turned)
    sums[BASIS + 32 : BASIS + 64] = by_block(block, [turned, inner[32:64], inner[32:64], pltpu.roll(last, 32, 1)])
    block = block[:16]
    sums[BASIS + 64 :] = by_block(
        block,
        [pltpu.roll(inner[64:80], 64, 1), pltpu.roll(inner[80:96], 96, 1), pltpu.roll(last[:16], 96, 1), last[16:]],
    )
    half = sums.shape[0] // 2
    even = owns_first_half()
    keep_ref[...] = pick(even, sums[:half], sums[half:])
    give_ref[...] = pick(even, sums[half:], sums[:half])


def by_block(block, values):
    return jnp.where(
        block < 2, jnp.where(block < 1, values[0], values[1]), jnp.where(block < 3, values[2], values[3])
    )


def unpack(sums):
    cross = sums[:BASIS]
    top, middle, tail = sums[BASIS : BASIS + 32], sums[BASIS + 32 : BASIS + 64], sums[BASIS + 64 : BASIS + 80]
    block = lane_of((BLOCK, LANES)) // BLOCK
    corner = jnp.concatenate([pltpu.roll(tail, 64, 1), pltpu.roll(tail, 32, 1)], axis=0)
    moment = jnp.concatenate([tail, pltpu.roll(tail, 96, 1)], axis=0)
    last = jnp.concatenate([pltpu.roll(tail, 32, 1), tail], axis=0)
    upper = jnp.concatenate([top, middle, corner, jnp.zeros((BLOCK, LANES), F32)], axis=0)
    row, lane = row_of((BASIS, LANES)) // BLOCK, lane_of((BASIS, LANES)) // BLOCK
    inner = jnp.where(row <= lane, upper[:BASIS], jnp.transpose(upper)[:BASIS])
    inner = jnp.where(lane < BASIS // BLOCK, inner, 0.0)
    moments = cross[BASIS - BLOCK :]
    half = pltpu.roll(moments, 64, 1)
    first = jnp.where(block == 0, moment, pltpu.roll(moments, 32, 1)) + pltpu.roll(moments, 96, 1)
    first = jnp.where(block == 3, top, first)
    second = jnp.where(block == 2, half + pltpu.roll(top, 96, 1), pltpu.roll(moment, 32, 1) + moments + half)
    second = jnp.where(block == 3, pltpu.roll(middle, 96, 1), second)
    third = jnp.where(block == 3, middle, corner + pltpu.roll(middle, 64, 1))
    return inner, cross, jnp.concatenate([first, second, third, last], axis=0)


def split_rows(values):
    high = values.astype(BF16).astype(F32)
    rest = values - high
    middle = rest.astype(BF16).astype(F32)
    low = rest - middle
    left = jnp.concatenate([high, high, middle, high, low, middle], axis=0).astype(BF16)
    right = jnp.concatenate([high, middle, high, low, high, middle], axis=0).astype(BF16)
    return left, right


def factor(joined, upper, inverse):
    count = upper.shape[0]
    shape = (SUBLANES, count)
    sub, lane = row_of(shape), lane_of(shape)
    panel = range(SUBLANES)
    entry = lambda rows, i, j: jnp.broadcast_to(rows[i : i + 1, j : j + 1], shape)
    spread = lambda rows: [jnp.broadcast_to(rows[i : i + 1], shape) for i in panel]

    def entries(rows, start):
        return {(i, j): entry(rows[i], 0, start + j) for i in panel for j in panel if j >= i}

    rows_a = spread(joined[:SUBLANES, :count])
    a = entries(rows_a, 0)
    for start in range(0, count, SUBLANES):
        stop = start + SUBLANES
        following = spread(joined[stop : stop + SUBLANES, :count]) if stop < count else None
        rows_b = spread(joined[start:stop, count:])
        for k in panel:
            scale = lax.rsqrt(a[k, k])
            rows_a[k], rows_b[k] = rows_a[k] * scale, rows_b[k] * scale
            scaled = {j: a[k, j] * scale for j in panel if j > k}
            for i in scaled:
                for j in panel:
                    if j >= i:
                        a[i, j] = a[i, j] - scaled[i] * scaled[j]
                rows_a[i] = rows_a[i] - scaled[i] * rows_a[k]
                rows_b[i] = rows_b[i] - scaled[i] * rows_b[k]
        out_a, out_b = rows_a[0], rows_b[0]
        for i in panel[1:]:
            out_a, out_b = jnp.where(sub == i, rows_a[i], out_a), jnp.where(sub == i, rows_b[i], out_b)
        out_a = jnp.where(lane >= sub + start, out_a, 0.0)
        upper[start:stop], inverse[start:stop] = out_a, out_b
        if stop == count:
            break
        for k in panel:
            for j in panel:
                following[j] = following[j] - entry(rows_a[k], 0, stop + j) * rows_a[k]
        rows_a, a = following, entries(following, stop)
        left, right = split_rows(jnp.concatenate([out_a, out_b], axis=1))
        update = lax.dot_general(left[:, :count], right, (((0,), (0,)), ((), ())), preferred_element_type=F32)
        after = stop + SUBLANES
        joined[stop:after, count:] = joined[stop:after, count:] - update[stop:after, count:]
        if after < count:
            joined[after:] = joined[after:] - update[after:]


def basis_change(centre, width):
    def apply_a(c):
        up = [0.0] + [width * v for v in c[:-1]]
        down = [width * v for v in c[1:]] + [0.0]
        return [centre * v + u + d for v, u, d in zip(c, up, down)]

    def apply_x(c):
        out = [0.0] * len(c)
        out[1] = out[1] + c[0]
        for k in range(1, len(c)):
            if k + 1 < len(c):
                out[k + 1] = out[k + 1] + 0.5 * c[k]
            out[k - 1] = out[k - 1] + 0.5 * c[k]
        return [(o - centre * v) * (1.0 / width) for o, v in zip(out, c)]

    one = centre * 0.0 + 1.0
    t = [[one] + [0.0] * POWERS]
    s = [[one] + [0.0] * POWERS]
    t.append(apply_a(t[0]))
    s.append(apply_x(s[0]))
    for _ in range(1, POWERS):
        t.append([2.0 * v - w for v, w in zip(apply_a(t[-1]), t[-2])])
        s.append([v - w for v, w in zip(apply_x(s[-1]), s[-2])])
    return t, s


def per_block(values):
    block = lane_of((SUBLANES, WIDE)) // BLOCK
    out = jnp.zeros((SUBLANES, WIDE), F32)
    for k, value in enumerate(values):
        out = jnp.where(block == k, value, out)
    return out[:1]


def finish_body(scale, shift_ref, q_ref, s_ref, mine_ref, other_ref, basis_ref, projection_ref, triangle_ref, joined, upper, inverse):
    size_x, size_y, width = basis_ref.shape
    size_z = width // WIDE
    even = owns_first_half()
    mine, other = mine_ref[...] * scale, other_ref[...] * scale
    sums = jnp.concatenate([pick(even, mine, other), pick(even, other, mine)], axis=0)

    centre, spread = shift_ref[0] * (1.0 / OPERATOR_SCALE) - 1.0, math.sqrt(DEGREE) / OPERATOR_SCALE
    t, s = basis_change(centre, spread)
    constant = per_block([t[k][0] for k in range(1, POWERS + 1)])
    removed = per_block([-s[k][0] for k in range(1, POWERS + 1)])
    mixes = [
        per_block([t[k][k - m] if k > m else 0.0 for k in range(1, POWERS + 1)]) for m in range(POWERS)
    ]

    def to_powers(values):
        total = values * mixes[0]
        for m in range(1, POWERS):
            total = total + pltpu.roll(values, m * BLOCK, 1) * mixes[m]
        return total

    inner, cross, square = unpack(sums)
    shape = inner.shape
    row, lane = row_of(shape), lane_of(shape)
    block = lane // BLOCK
    defect = jnp.where(row == lane, 1.0, 0.0) - inner
    first = (BASIS - BLOCK) // BLOCK
    copies = [pltpu.roll(defect, ((k - first) * BLOCK) % WIDE, 1) if k != first else defect for k in range(POWERS)]
    start = jnp.where(block < 2, jnp.where(block < 1, copies[0], copies[1]), jnp.where(block < 3, copies[2], copies[3]))
    parts = jnp.concatenate(halves(defect), axis=1)
    pad = lambda values: jnp.concatenate([values, jnp.zeros((LANES - BASIS, WIDE), F32)], axis=0)
    by_defect = lambda values: wide_dot(parts, stacked(pad(values)))
    start_removed = start * removed
    change = by_defect(cross - start_removed)
    moved = cross + change
    left = by_defect(start_removed + change)
    product = contract_parts(
        jnp.concatenate(halves(jnp.concatenate([cross, moved], axis=0)), axis=1),
        jnp.concatenate(halves(jnp.concatenate([moved, left], axis=0)), axis=1),
    )
    start_unit = jnp.where(row - (BASIS - BLOCK) == lane - block * BLOCK, 1.0, 0.0)
    both = cross + by_defect(cross)
    projection_ref[...] = to_powers(both) + (start_unit - by_defect(start)) * constant
    joined[:, :WIDE] = square - product
    shape = (WIDE, WIDE)
    joined[:, WIDE:] = jnp.where(row_of(shape) == lane_of(shape), 1.0, 0.0)
    twice = s_ref[...] - wide_dot(q_ref[...], stacked(pad(moved)))
    twice_parts = jnp.concatenate(halves(twice), axis=1)
    factor(joined, upper, inverse)
    triangle_ref[...] = to_powers(upper[...])
    solve = stacked(jnp.transpose(inverse[...]))
    new_basis = wide_dot(twice_parts, solve)
    for i in range(size_x):
        for k in range(size_z):
            at = (i * size_z + k) * size_y
            basis_ref[i, :, k * WIDE : (k + 1) * WIDE] = new_basis[at : at + size_y]


def reduced(keep, give):
    sizes = [lax.axis_size(axis) for axis in AXES]
    if sizes[0] < 2 or any(size & (size - 1) for size in sizes):
        even = owns_first_half()
        whole = jnp.concatenate([pick(even, keep, give), pick(even, give, keep)], axis=0)
        first, second = jnp.split(lax.psum(whole, AXES), 2)
        return pick(even, first, second), pick(even, second, first)
    place = lambda at: (at[0] * sizes[1] + at[1]) * sizes[2] + at[2]
    devices = [(i, j, k) for i in range(sizes[0]) for j in range(sizes[1]) for k in range(sizes[2])]

    def swap(values, flips):
        links = [(place(at), place([a ^ b for a, b in zip(at, flips)])) for at in devices]
        return lax.ppermute(values, AXES, links)

    total = keep + swap(give, (1, 0, 0))
    for axis in ("gx", "gz", "gy"):
        for k in bits(axis):
            if (axis, k) != ("gx", 0):
                flips = [(1 << k) * (name == axis) for name in AXES]
                flips[0] ^= 1
                total = total + swap(total, flips)
    return total, swap(total, (1, 0, 0))


def exchange(first, second, axis, helper):
    count, others = lax.axis_size(axis), lax.axis_size(helper)
    near = [(i, i + 1) for i in range(0, count - 1, 2)]
    far = [(i, i + 1) for i in range(1, count - 1, 2)]
    axes = tuple(name for name in AXES if name in (axis, helper))
    place = lambda at: at[0] * others + at[1] if axes[0] == axis else at[1] * count + at[0]
    got = []
    for value, pairs in ((first, near), (second, far)):
        if not pairs:
            continue
        links = [((i, k), (j, k)) for pair in pairs for i, j in (pair, pair[::-1]) for k in range(others)]
        if others % 2 == 0:
            alone = [i for i in range(count) if not any(i in pair for pair in pairs)]
            links += [((i, k), (i, k ^ 1)) for i in alone for k in range(others)]
        got.append(lax.ppermute(value, axes, [(place(source), place(target)) for source, target in links]))
    return got


def filled(halos, like):
    return halos + [jnp.zeros_like(like)] * (2 - len(halos))


def cycle(prior_basis, edge_weights, spectral_shift):
    size_x, size_y, _ = prior_basis.shape
    size_z = prior_basis.shape[2] // BASIS
    own = size_z * BLOCK
    cell_local = size_x * size_y * size_z
    cell_count = cell_local
    for axis in AXES:
        cell_count = cell_count * lax.axis_size(axis)

    hbm = pl.BlockSpec(memory_space=pltpu.HBM)
    faces = min(lax.axis_size("gz") - 1, 2)
    field, *faces = kernel_call(
        pack_body,
        [(size_x, size_y, own + LANES)] + [(size_x, size_y, 2 * LANES)] * faces,
        [
            pltpu.VMEM(prior_basis.shape, F32),
            pltpu.VMEM(edge_weights.shape, F32),
            pltpu.SemaphoreType.DMA((size_x,)),
            pltpu.SemaphoreType.DMA(()),
        ],
        [hbm, hbm],
    )(*(pltpu.with_memory_space_constraint(array, pltpu.HBM) for array in (prior_basis, edge_weights)))
    halos = exchange(faces[0], faces[-1], "gz", "gx") if faces else []
    planes_x = filled(exchange(field, field, "gx", "gz"), field)
    degree_shift = spectral_shift + DEGREE
    prior_rows, prior_parts, inner = kernel_call(
        prior_body,
        [(cell_local, LANES), jax.ShapeDtypeStruct((cell_local, 2 * LANES), BF16), (BASIS, LANES)],
        cost=pl.CostEstimate(flops=6 * 2 * cell_local * LANES * LANES, bytes_accessed=4 * prior_basis.size, transcendentals=0),
    )(prior_basis)
    width = own + 3 * LANES
    side = (POWERS - 1, size_y, 3 * LANES)
    wide, first, second, *side_faces = kernel_call(
        widen_body, [(size_x, size_y, width)] + [(size_x, POWERS, width)] * 2 + [side] * 2
    )(field, *halos)
    halos = filled(exchange(first, second, "gy", "gx"), first)
    sides_x = filled(exchange(*side_faces, "gx", "gz"), side_faces[0])
    rest = (POWERS - 1, 2 * POWERS, width)
    long, first, second = kernel_call(lengthen_body, [(size_x, size_y + 2 * POWERS, width), rest, rest])(wide, *halos)
    rests = filled(exchange(first, second, "gx", "gz"), first)

    rows, planes, lanes = size_y + 2 * POWERS, size_x + 2 * POWERS, own + 2 * LANES
    sum_rows = BASIS + 80
    half = (sum_rows // 2, WIDE)
    columns, keep, give = kernel_call(
        functools.partial(columns_body, size_z),
        [(cell_local, WIDE), half, half],
        [
            pltpu.VMEM((planes, rows, width), F32),
            pltpu.VMEM((3, planes, rows, lanes), F32),
            pltpu.VMEM((planes, rows, lanes), F32),
            pltpu.VMEM((POWERS, planes, rows, lanes), F32),
            pltpu.VMEM((sum_rows, WIDE), F32),
            pltpu.VMEM((cell_local, 2 * LANES), BF16),
            pltpu.VMEM((cell_local, 2 * WIDE), BF16),
        ],
    )(long, *planes_x, *sides_x, *rests, prior_rows, inner)

    total, other = reduced(keep, give)

    new_basis, projection, triangle = pl.pallas_call(
        functools.partial(finish_body, 1.0 / cell_count),
        in_specs=[pl.BlockSpec(memory_space=pltpu.SMEM)] + [pl.BlockSpec(memory_space=pltpu.VMEM)] * 4,
        out_shape=[
            jax.ShapeDtypeStruct((size_x, size_y, size_z * WIDE), F32),
            jax.ShapeDtypeStruct((BASIS, WIDE), F32),
            jax.ShapeDtypeStruct((WIDE, WIDE), F32),
        ],
        scratch_shapes=[
            pltpu.VMEM((WIDE, 2 * WIDE), F32),
            pltpu.VMEM((WIDE, WIDE), F32),
            pltpu.VMEM((WIDE, WIDE), F32),
        ],
        compiler_params=pltpu.CompilerParams(vmem_limit_bytes=24 * 1024 * 1024),
    )(degree_shift, prior_parts, columns, total, other)
    return new_basis, projection, triangle


def solution(mesh):
    return jax.shard_map(
        cycle,
        mesh=mesh,
        in_specs=(P("gx", "gy", "gz"), P(None, "gx", "gy", "gz"), P()),
        out_specs=(P("gx", "gy", "gz"), P(), P()),
        check_vma=False,
    )
```

```python
import functools
import math

import jax
import jax.numpy as jnp
from jax import lax
from jax.experimental import pallas as pl
from jax.experimental.pallas import tpu as pltpu
from jax.sharding import PartitionSpec as P


BLOCK = 32
POWERS = 4
BASIS = 96
WIDE = BLOCK * POWERS

PRECISE = lax.Precision.HIGHEST
OPERATOR_SCALE = 11.0
DEGREE = 6.0
LANES = 128
SUBLANES = 8
EARLY = 4
F32 = jnp.float32
BF16 = jnp.bfloat16
AXES = ("gx", "gy", "gz")


def lane_of(shape):
    return lax.broadcasted_iota(jnp.int32, shape, 1)


def row_of(shape):
    return lax.broadcasted_iota(jnp.int32, shape, 0)


def kernel_call(body, shapes, scratch=(), in_specs=None, cost=None, limit=24 * 1024 * 1024):
    options = {} if in_specs is None else {"in_specs": in_specs}
    return pl.pallas_call(
        body,
        out_shape=[shape if isinstance(shape, jax.ShapeDtypeStruct) else jax.ShapeDtypeStruct(shape, F32) for shape in shapes],
        scratch_shapes=list(scratch),
        compiler_params=pltpu.CompilerParams(vmem_limit_bytes=limit),
        cost_estimate=cost,
        **options,
    )


def even_on(axis):
    return lax.axis_index(axis) % 2 == 0


def last_on(axis):
    return lax.axis_index(axis) == lax.axis_size(axis) - 1


def sides(axis, first, second):
    even = even_on(axis)
    above = jnp.where(last_on(axis), 0.0, jnp.where(even, first, second))
    below = jnp.where(lax.axis_index(axis) == 0, 0.0, jnp.where(even, second, first))
    return above, below


def bits(axis):
    return range((lax.axis_size(axis) - 1).bit_length())


def owns_first_half():
    ones = sum((lax.axis_index(axis) >> k) & 1 for axis in AXES for k in bits(axis))
    return ones % 2 == 0


def pick(even, first, second):
    return jnp.where(even, first, second)


def pack_body(prior_hbm, weights_hbm, field_ref, *refs):
    face_refs, (prior_ref, weights_ref, prior_sem, weights_sem) = refs[:-4], refs[-4:]
    size_x, size_y, width = field_ref.shape
    weights_copy = pltpu.make_async_copy(weights_hbm, weights_ref, weights_sem)
    copies = [pltpu.make_async_copy(prior_hbm.at[i], prior_ref.at[i], prior_sem.at[i]) for i in range(size_x)]
    weights_copy.start()
    for copy in copies:
        copy.start()
    own = width - LANES
    size_z = own // BLOCK
    shape = (size_y, LANES)
    lane = lane_of(shape)
    even = even_on("gz")
    weights_copy.wait()
    for i in range(size_x):
        pieces = [weights_ref[d, i] for d in range(3)]
        pieces.append(jnp.zeros((size_y, LANES - 3 * size_z), F32))
        weights = jnp.concatenate(pieces, axis=1)
        field_ref[i, :, own:] = weights
        for face_ref in face_refs:
            face_ref[i, :, LANES:] = weights
    for i in range(size_x):
        copies[i].wait()
        values = []
        for q in range(own // LANES):
            tiles = [prior_ref[i, :, (3 * q + m) * LANES : (3 * q + m + 1) * LANES] for m in range(3)]
            low, high = pltpu.roll(tiles[0], 64, 1), pltpu.roll(tiles[2], 64, 1)
            value = jnp.where(lane < 64, jnp.where(lane < 32, low, tiles[1]), jnp.where(lane < 96, high, tiles[2]))
            field_ref[i, :, q * LANES : (q + 1) * LANES] = value
            values.append(value)
        faces = [pick(even, values[-1], values[0]), pick(even, values[0], values[-1])]
        for face_ref, face in zip(face_refs, faces):
            face_ref[i, :, :LANES] = face


def nearest(planes, refs):
    even = even_on("gx")
    for at in range(POWERS - 1):
        low, high = planes[at], planes[len(planes) - POWERS + 1 + at]
        refs[0][at] = pick(even, high, low)
        refs[1][at] = pick(even, low, high)


def widen_body(field_ref, *refs):
    halo_refs, (wide_ref, *face_refs) = refs[:-5], refs[-5:]
    size_x, size_y, width = field_ref.shape
    own = width - LANES
    size_z = own // BLOCK
    lane = lane_of((size_y, LANES))
    upper = (lane % size_z) < size_z // 2
    even_y = even_on("gy")
    zero = jnp.zeros((size_y, LANES), F32)
    side = []
    for i in range(size_x):
        values = [ref[i, :, :LANES] for ref in halo_refs] + [zero, zero]
        others = [ref[i, :, LANES:] for ref in halo_refs] + [zero, zero]
        above, below = sides("gz", values[0], values[1])
        above_w, below_w = sides("gz", others[0], others[1])
        other = pltpu.roll(jnp.where(upper, above_w, below_w), 3 * size_z, 1)
        weights = jnp.where(lane < 3 * size_z, field_ref[i, :, own:], jnp.where(lane < 6 * size_z, other, zero))
        row = jnp.concatenate([field_ref[i, :, :own], above, below, weights], axis=1)
        wide_ref[i] = row
        low, high = row[:POWERS], row[size_y - POWERS :]
        face_refs[0][i] = pick(even_y, high, low)
        face_refs[1][i] = pick(even_y, low, high)
        side.append(row[:, own:])
    nearest(side, face_refs[2:])


def lengthen_body(wide_ref, first_ref, second_ref, long_ref, *rest_refs):
    size_x, size_y, _ = wide_ref.shape
    rest = []
    for i in range(size_x):
        long_ref[i, :size_y] = wide_ref[i]
        halo = jnp.concatenate(sides("gy", first_ref[i], second_ref[i]), axis=0)
        long_ref[i, size_y:] = halo
        rest.append(halo)
    nearest(rest, rest_refs)


def contract(left, right):
    return lax.dot_general(
        left, right, (((0,), (0,)), ((), ())), precision=PRECISE, preferred_element_type=F32
    )


def prior_body(prior_ref, q_ref, parts_ref, inner_ref, selector_ref):
    size_x, size_y, width = prior_ref.shape
    size_z = width // BASIS
    lane = lane_of((size_y, LANES))
    for i in range(size_x):
        for q in range(width // (3 * LANES)):
            prior = [prior_ref[i, :, (3 * q + m) * LANES : (3 * q + m + 1) * LANES] for m in range(3)]
            rows = [
                prior[0],
                jnp.where(lane < 32, pltpu.roll(prior[0], 32, 1), pltpu.roll(prior[1], 32, 1)),
                jnp.where(lane < 64, pltpu.roll(prior[1], 64, 1), pltpu.roll(prior[2], 64, 1)),
                pltpu.roll(prior[2], 96, 1),
            ]
            for r in range(4):
                at = (i * size_z + 4 * q + r) * size_y
                q_ref[at : at + size_y] = jnp.where(lane < BASIS, rows[r], 0.0)
    rows = q_ref[...]
    field = selector_ref.shape[2]
    source = row_of((LANES, field))
    position = lane_of((LANES, field)) // BLOCK
    place = jnp.where(
        position < size_z,
        position,
        jnp.where(position < size_z + POWERS, position + 2 * size_z, position + 3 * size_z - 2 * POWERS),
    )
    for d in range(3):
        selector_ref[d] = jnp.where(source == place + d * size_z, 1.0, 0.0).astype(BF16)
    inner_ref[...] = contract(rows, rows)[:BASIS]
    parts_ref[:, :LANES], parts_ref[:, LANES:] = halves(rows)


def halves(values):
    high = values.astype(BF16)
    return high, (values - high.astype(F32)).astype(BF16)


def stacked(right):
    high, low = halves(right)
    return jnp.concatenate(
        [jnp.concatenate([high, low], axis=1), jnp.concatenate([high, jnp.zeros_like(low)], axis=1)], axis=0
    )


def wide_dot(left_parts, right):
    both = jnp.dot(left_parts, right, preferred_element_type=F32)
    count = right.shape[1] // 2
    return both[:, :count] + both[:, count:]


def contract_parts(left, right):
    product = lax.dot_general(left, right, (((0,), (0,)), ((), ())), preferred_element_type=F32)
    rows, columns = left.shape[1] // 2, right.shape[1] // 2
    product = product[:rows] + product[rows:]
    return product[:, :columns] + product[:, columns:]


def columns_body(size_z, own_ref, near_ref, far_ref, near_side_ref, far_side_ref, near_rest_ref, far_rest_ref, q_ref, inner_ref, selector_ref, s_ref, keep_ref, give_ref, joined, coupling, diagonal, levels, sums, q_parts, s_parts):
    size_x, rows, width = own_ref.shape
    size_y = rows - 2 * POWERS
    field = width - LANES
    own = size_z * BLOCK
    planes = size_x + 2 * POWERS
    joined[:size_x] = own_ref[...]
    for at in range(POWERS):
        high = near_ref.shape[0] - POWERS + at
        above, _ = sides("gx", near_ref[at], far_ref[at])
        _, below = sides("gx", near_ref[high], far_ref[high])
        for p, value in ((size_x + at, above), (size_x + POWERS + at, below)):
            joined[p, :size_y, :own] = value[:, :own]
            joined[p, :size_y, field:] = value[:, own:]
    zero = jnp.zeros((size_y, 2 * LANES), F32)
    for p in (size_x + POWERS - 1, size_x + POWERS):
        joined[p, :size_y, own:field] = zero
        joined[p, size_y:] = jnp.zeros((2 * POWERS, width), F32)
    for at in range(POWERS - 1):
        halo = sides("gx", near_rest_ref[at], far_rest_ref[at])
        side = sides("gx", near_side_ref[at], far_side_ref[at])
        for up in range(2):
            p = size_x + at + up * (POWERS + 1)
            joined[p, :size_y, own:] = side[up]
            joined[p, size_y:] = halo[up]

    weights = joined[:, :, field:].reshape(-1, LANES)
    weights = jnp.concatenate(halves(weights * (1.0 / math.sqrt(DEGREE))), axis=1)
    for d in range(3):
        selector = jnp.concatenate([selector_ref[d]] * 2, axis=0)
        spread = jnp.dot(weights, selector, preferred_element_type=F32)
        coupling[d] = spread.reshape(planes, rows, field)
    row_last = (row_of((rows, field)) == size_y - 1) & last_on("gy")
    lane_last = (lane_of((rows, field)) // BLOCK == size_z - 1) & last_on("gz")

    distance = lambda p: 0 if p < size_x else min(p - size_x + 1, planes - p)
    near = lambda layers: [p for p in range(planes) if p < size_x + layers or p >= planes - layers]
    for p in near(POWERS - 1):
        x, y, z = (coupling[d, p] for d in range(3))
        x_low = coupling[0, (p - 1) % planes]
        diagonal[p] = x + x_low + (y + pltpu.roll(y, 1, 0)) + (z + pltpu.roll(z, BLOCK, 1)) - math.sqrt(DEGREE)
    for p in near(POWERS - 1):
        coupling[1, p] = jnp.where(row_last, 0.0, coupling[1, p])
        coupling[2, p] = jnp.where(lane_last, 0.0, coupling[2, p])
    coupling[0, size_x - 1] = jnp.where(last_on("gx"), 0.0, coupling[0, size_x - 1])

    def level(k, p):
        return joined[p, :, :field] if k == 0 else levels[k - 1, p]

    for k in range(1, POWERS + 1):
        for p in near(POWERS - k):
            value = level(k - 1, p)
            up, down = (p + 1) % planes, (p - 1) % planes
            x, y, z = (coupling[d, p] for d in range(3))
            total = diagonal[p] * value - x * level(k - 1, up) - coupling[0, down] * level(k - 1, down)
            total = total - y * pltpu.roll(value, rows - 1, 0) - pltpu.roll(y * value, 1, 0)
            total = total - z * pltpu.roll(value, field - BLOCK, 1) - pltpu.roll(z * value, BLOCK, 1)
            if k > 1:
                total = total - level(k - 2, p)
            reach = POWERS - k - distance(p)
            if reach == 0:
                levels[k - 1, p, :size_y, :own] = total[:size_y, :own]
            elif reach == 1:
                levels[k - 1, p, :size_y] = total[:size_y]
                levels[k - 1, p, size_y:, :own] = total[size_y:, :own]
            else:
                levels[k - 1, p] = total

    lane = lane_of((size_y, LANES))
    block = lane // BLOCK
    for i in range(size_x):
        for q in range(own // LANES):
            tiles = [levels[m, i, :size_y, q * LANES : (q + 1) * LANES] for m in range(POWERS)]
            for r in range(4):
                moved = [pltpu.roll(tiles[m], (32 * (m - r)) % LANES, 1) if m != r else tiles[m] for m in range(POWERS)]
                at = (i * size_z + 4 * q + r) * size_y
                row = by_block(block, moved)
                s_ref[at : at + size_y] = row
                s_parts[at : at + size_y, :WIDE], s_parts[at : at + size_y, WIDE:] = halves(row)
                row = jnp.where(lane < BASIS, q_ref[at : at + size_y], row)
                q_parts[at : at + size_y, :LANES], q_parts[at : at + size_y, LANES:] = halves(row)

    product = contract_parts(q_parts[...], s_parts[...])
    sums[:BASIS] = product[:BASIS]
    last = product[BASIS:]
    inner = inner_ref[...]
    block = lane_of((BLOCK, LANES)) // BLOCK
    turned = pltpu.roll(last, 96, 1)
    sums[BASIS : BASIS + 32] = jnp.where(block < 3, inner[:32], turned)
    sums[BASIS + 32 : BASIS + 64] = by_block(block, [turned, inner[32:64], inner[32:64], pltpu.roll(last, 32, 1)])
    block = block[:16]
    sums[BASIS + 64 :] = by_block(
        block,
        [pltpu.roll(inner[64:80], 64, 1), pltpu.roll(inner[80:96], 96, 1), pltpu.roll(last[:16], 96, 1), last[16:]],
    )
    half = sums.shape[0] // 2
    even = owns_first_half()
    keep_ref[...] = pick(even, sums[:half], sums[half:])
    give_ref[...] = pick(even, sums[half:], sums[:half])


def by_block(block, values):
    return jnp.where(
        block < 2, jnp.where(block < 1, values[0], values[1]), jnp.where(block < 3, values[2], values[3])
    )


def unpack(sums):
    cross = sums[:BASIS]
    top, middle, tail = sums[BASIS : BASIS + 32], sums[BASIS + 32 : BASIS + 64], sums[BASIS + 64 : BASIS + 80]
    block = lane_of((BLOCK, LANES)) // BLOCK
    corner = jnp.concatenate([pltpu.roll(tail, 64, 1), pltpu.roll(tail, 32, 1)], axis=0)
    moment = jnp.concatenate([tail, pltpu.roll(tail, 96, 1)], axis=0)
    last = jnp.concatenate([pltpu.roll(tail, 32, 1), tail], axis=0)
    upper = jnp.concatenate([top, middle, corner, jnp.zeros((BLOCK, LANES), F32)], axis=0)
    row, lane = row_of((BASIS, LANES)) // BLOCK, lane_of((BASIS, LANES)) // BLOCK
    inner = jnp.where(row <= lane, upper[:BASIS], jnp.transpose(upper)[:BASIS])
    inner = jnp.where(lane < BASIS // BLOCK, inner, 0.0)
    moments = cross[BASIS - BLOCK :]
    half = pltpu.roll(moments, 64, 1)
    first = jnp.where(block == 0, moment, pltpu.roll(moments, 32, 1)) + pltpu.roll(moments, 96, 1)
    first = jnp.where(block == 3, top, first)
    second = jnp.where(block == 2, half + pltpu.roll(top, 96, 1), pltpu.roll(moment, 32, 1) + moments + half)
    second = jnp.where(block == 3, pltpu.roll(middle, 96, 1), second)
    third = jnp.where(block == 3, middle, corner + pltpu.roll(middle, 64, 1))
    return inner, cross, jnp.concatenate([first, second, third, last], axis=0)


def split_rows(values):
    high = values.astype(BF16).astype(F32)
    rest = values - high
    middle = rest.astype(BF16).astype(F32)
    low = rest - middle
    left = jnp.concatenate([high, high, middle, high, low, middle], axis=0).astype(BF16)
    right = jnp.concatenate([high, middle, high, low, high, middle], axis=0).astype(BF16)
    return left, right


def factor(joined, upper, inverse):
    count = upper.shape[0]
    shape = (SUBLANES, count)
    sub, lane = row_of(shape), lane_of(shape)
    panel = range(SUBLANES)
    entry = lambda rows, i, j: jnp.broadcast_to(rows[i : i + 1, j : j + 1], shape)
    spread = lambda rows: [jnp.broadcast_to(rows[i : i + 1], shape) for i in panel]

    def entries(rows, start):
        return {(i, j): entry(rows[i], 0, start + j) for i in panel for j in panel if j >= i}

    rows_a = spread(joined[:SUBLANES, :count])
    a = entries(rows_a, 0)
    for start in range(0, count, SUBLANES):
        stop = start + SUBLANES
        following = spread(joined[stop : stop + SUBLANES, :count]) if stop < count else None
        rows_b = spread(joined[start:stop, count:])
        for k in panel:
            scale = lax.rsqrt(a[k, k])
            rows_a[k], rows_b[k] = rows_a[k] * scale, rows_b[k] * scale
            scaled = {j: a[k, j] * scale for j in panel if j > k}
            for i in scaled:
                for j in panel:
                    if j >= i:
                        a[i, j] = a[i, j] - scaled[i] * scaled[j]
                rows_a[i] = rows_a[i] - scaled[i] * rows_a[k]
                rows_b[i] = rows_b[i] - scaled[i] * rows_b[k]
        out_a, out_b = rows_a[0], rows_b[0]
        for i in panel[1:]:
            out_a, out_b = jnp.where(sub == i, rows_a[i], out_a), jnp.where(sub == i, rows_b[i], out_b)
        out_a = jnp.where(lane >= sub + start, out_a, 0.0)
        upper[start:stop], inverse[start:stop] = out_a, out_b
        if stop == count:
            break
        for k in panel:
            factors = [entry(rows_a[k], 0, stop + j) for j in panel]
            for j in panel:
                following[j] = following[j] - factors[j] * rows_a[k]
            if k + 1 == EARLY:
                a = entries(following, stop)
            elif k + 1 > EARLY:
                a = {(i, j): value - factors[i] * factors[j] for (i, j), value in a.items()}
        rows_a = following
        left, right = split_rows(jnp.concatenate([out_a, out_b], axis=1))
        update = lax.dot_general(left[:, :count], right, (((0,), (0,)), ((), ())), preferred_element_type=F32)
        after = stop + SUBLANES
        joined[stop:after, count:] = joined[stop:after, count:] - update[stop:after, count:]
        if after < count:
            joined[after:] = joined[after:] - update[after:]


def basis_change(centre, width):
    def apply_a(c):
        up = [0.0] + [width * v for v in c[:-1]]
        down = [width * v for v in c[1:]] + [0.0]
        return [centre * v + u + d for v, u, d in zip(c, up, down)]

    def apply_x(c):
        out = [0.0] * len(c)
        out[1] = out[1] + c[0]
        for k in range(1, len(c)):
            if k + 1 < len(c):
                out[k + 1] = out[k + 1] + 0.5 * c[k]
            out[k - 1] = out[k - 1] + 0.5 * c[k]
        return [(o - centre * v) * (1.0 / width) for o, v in zip(out, c)]

    one = centre * 0.0 + 1.0
    t = [[one] + [0.0] * POWERS]
    s = [[one] + [0.0] * POWERS]
    t.append(apply_a(t[0]))
    s.append(apply_x(s[0]))
    for _ in range(1, POWERS):
        t.append([2.0 * v - w for v, w in zip(apply_a(t[-1]), t[-2])])
        s.append([v - w for v, w in zip(apply_x(s[-1]), s[-2])])
    return t, s


def per_block(values):
    block = lane_of((SUBLANES, WIDE)) // BLOCK
    out = jnp.zeros((SUBLANES, WIDE), F32)
    for k, value in enumerate(values):
        out = jnp.where(block == k, value, out)
    return out[:1]


def finish_body(scale, shift_ref, q_ref, s_ref, mine_ref, other_ref, basis_ref, projection_ref, triangle_ref, joined, upper, inverse):
    size_x, size_y, width = basis_ref.shape
    size_z = width // WIDE
    even = owns_first_half()
    mine, other = mine_ref[...] * scale, other_ref[...] * scale
    sums = jnp.concatenate([pick(even, mine, other), pick(even, other, mine)], axis=0)

    centre, spread = shift_ref[0] * (1.0 / OPERATOR_SCALE) - 1.0, math.sqrt(DEGREE) / OPERATOR_SCALE
    t, s = basis_change(centre, spread)
    constant = per_block([t[k][0] for k in range(1, POWERS + 1)])
    removed = per_block([-s[k][0] for k in range(1, POWERS + 1)])
    mixes = [
        per_block([t[k][k - m] if k > m else 0.0 for k in range(1, POWERS + 1)]) for m in range(POWERS)
    ]

    def to_powers(values):
        total = values * mixes[0]
        for m in range(1, POWERS):
            total = total + pltpu.roll(values, m * BLOCK, 1) * mixes[m]
        return total

    inner, cross, square = unpack(sums)
    shape = inner.shape
    row, lane = row_of(shape), lane_of(shape)
    block = lane // BLOCK
    defect = jnp.where(row == lane, 1.0, 0.0) - inner
    first = (BASIS - BLOCK) // BLOCK
    copies = [pltpu.roll(defect, ((k - first) * BLOCK) % WIDE, 1) if k != first else defect for k in range(POWERS)]
    start = jnp.where(block < 2, jnp.where(block < 1, copies[0], copies[1]), jnp.where(block < 3, copies[2], copies[3]))
    parts = jnp.concatenate(halves(defect), axis=1)
    pad = lambda values: jnp.concatenate([values, jnp.zeros((LANES - BASIS, WIDE), F32)], axis=0)
    by_defect = lambda values: wide_dot(parts, stacked(pad(values)))
    start_removed = start * removed
    change = by_defect(cross - start_removed)
    moved = cross + change
    left = by_defect(start_removed + change)
    product = contract_parts(
        jnp.concatenate(halves(jnp.concatenate([cross, moved], axis=0)), axis=1),
        jnp.concatenate(halves(jnp.concatenate([moved, left], axis=0)), axis=1),
    )
    start_unit = jnp.where(row - (BASIS - BLOCK) == lane - block * BLOCK, 1.0, 0.0)
    both = cross + by_defect(cross)
    projection_ref[...] = to_powers(both) + (start_unit - by_defect(start)) * constant
    joined[:, :WIDE] = square - product
    shape = (WIDE, WIDE)
    joined[:, WIDE:] = jnp.where(row_of(shape) == lane_of(shape), 1.0, 0.0)
    twice = s_ref[...] - wide_dot(q_ref[...], stacked(pad(moved)))
    twice_parts = jnp.concatenate(halves(twice), axis=1)
    factor(joined, upper, inverse)
    triangle_ref[...] = to_powers(upper[...])
    solve = stacked(jnp.transpose(inverse[...]))
    new_basis = wide_dot(twice_parts, solve)
    for i in range(size_x):
        for k in range(size_z):
            at = (i * size_z + k) * size_y
            basis_ref[i, :, k * WIDE : (k + 1) * WIDE] = new_basis[at : at + size_y]


def reduced(keep, give):
    sizes = [lax.axis_size(axis) for axis in AXES]
    if sizes[0] < 2 or any(size & (size - 1) for size in sizes):
        even = owns_first_half()
        whole = jnp.concatenate([pick(even, keep, give), pick(even, give, keep)], axis=0)
        first, second = jnp.split(lax.psum(whole, AXES), 2)
        return pick(even, first, second), pick(even, second, first)
    place = lambda at: (at[0] * sizes[1] + at[1]) * sizes[2] + at[2]
    devices = [(i, j, k) for i in range(sizes[0]) for j in range(sizes[1]) for k in range(sizes[2])]

    def swap(values, flips):
        links = [(place(at), place([a ^ b for a, b in zip(at, flips)])) for at in devices]
        return lax.ppermute(values, AXES, links)

    total = keep + swap(give, (1, 0, 0))
    for axis in ("gx", "gz", "gy"):
        for k in bits(axis):
            if (axis, k) != ("gx", 0):
                flips = [(1 << k) * (name == axis) for name in AXES]
                flips[0] ^= 1
                total = total + swap(total, flips)
    return total, swap(total, (1, 0, 0))


def exchange(first, second, axis, helper):
    count, others = lax.axis_size(axis), lax.axis_size(helper)
    near = [(i, i + 1) for i in range(0, count - 1, 2)]
    far = [(i, i + 1) for i in range(1, count - 1, 2)]
    axes = tuple(name for name in AXES if name in (axis, helper))
    place = lambda at: at[0] * others + at[1] if axes[0] == axis else at[1] * count + at[0]
    got = []
    for value, pairs in ((first, near), (second, far)):
        if not pairs:
            continue
        links = [((i, k), (j, k)) for pair in pairs for i, j in (pair, pair[::-1]) for k in range(others)]
        if others % 2 == 0:
            alone = [i for i in range(count) if not any(i in pair for pair in pairs)]
            links += [((i, k), (i, k ^ 1)) for i in alone for k in range(others)]
        got.append(lax.ppermute(value, axes, [(place(source), place(target)) for source, target in links]))
    return got


def filled(halos, like):
    return halos + [jnp.zeros_like(like)] * (2 - len(halos))


def cycle(prior_basis, edge_weights, spectral_shift):
    size_x, size_y, _ = prior_basis.shape
    size_z = prior_basis.shape[2] // BASIS
    own = size_z * BLOCK
    cell_local = size_x * size_y * size_z
    cell_count = cell_local
    for axis in AXES:
        cell_count = cell_count * lax.axis_size(axis)

    hbm = pl.BlockSpec(memory_space=pltpu.HBM)
    faces = min(lax.axis_size("gz") - 1, 2)
    field, *faces = kernel_call(
        pack_body,
        [(size_x, size_y, own + LANES)] + [(size_x, size_y, 2 * LANES)] * faces,
        [
            pltpu.VMEM(prior_basis.shape, F32),
            pltpu.VMEM(edge_weights.shape, F32),
            pltpu.SemaphoreType.DMA((size_x,)),
            pltpu.SemaphoreType.DMA(()),
        ],
        [hbm, hbm],
    )(*(pltpu.with_memory_space_constraint(array, pltpu.HBM) for array in (prior_basis, edge_weights)))
    halos = exchange(faces[0], faces[-1], "gz", "gx") if faces else []
    planes_x = filled(exchange(field, field, "gx", "gz"), field)
    degree_shift = spectral_shift + DEGREE
    prior_rows, prior_parts, inner, selector = kernel_call(
        prior_body,
        [
            (cell_local, LANES),
            jax.ShapeDtypeStruct((cell_local, 2 * LANES), BF16),
            (BASIS, LANES),
            jax.ShapeDtypeStruct((3, LANES, own + 2 * LANES), BF16),
        ],
        cost=pl.CostEstimate(flops=6 * 2 * cell_local * LANES * LANES, bytes_accessed=4 * prior_basis.size, transcendentals=0),
    )(prior_basis)
    width = own + 3 * LANES
    side = (POWERS - 1, size_y, 3 * LANES)
    wide, first, second, *side_faces = kernel_call(
        widen_body, [(size_x, size_y, width)] + [(size_x, POWERS, width)] * 2 + [side] * 2
    )(field, *halos)
    halos = filled(exchange(first, second, "gy", "gx"), first)
    sides_x = filled(exchange(*side_faces, "gx", "gz"), side_faces[0])
    rest = (POWERS - 1, 2 * POWERS, width)
    long, first, second = kernel_call(lengthen_body, [(size_x, size_y + 2 * POWERS, width), rest, rest])(wide, *halos)
    rests = filled(exchange(first, second, "gx", "gz"), first)

    rows, planes, lanes = size_y + 2 * POWERS, size_x + 2 * POWERS, own + 2 * LANES
    sum_rows = BASIS + 80
    half = (sum_rows // 2, WIDE)
    columns, keep, give = kernel_call(
        functools.partial(columns_body, size_z),
        [(cell_local, WIDE), half, half],
        [
            pltpu.VMEM((planes, rows, width), F32),
            pltpu.VMEM((3, planes, rows, lanes), F32),
            pltpu.VMEM((planes, rows, lanes), F32),
            pltpu.VMEM((POWERS, planes, rows, lanes), F32),
            pltpu.VMEM((sum_rows, WIDE), F32),
            pltpu.VMEM((cell_local, 2 * LANES), BF16),
            pltpu.VMEM((cell_local, 2 * WIDE), BF16),
        ],
    )(long, *planes_x, *sides_x, *rests, prior_rows, inner, selector)

    total, other = reduced(keep, give)

    new_basis, projection, triangle = pl.pallas_call(
        functools.partial(finish_body, 1.0 / cell_count),
        in_specs=[pl.BlockSpec(memory_space=pltpu.SMEM)] + [pl.BlockSpec(memory_space=pltpu.VMEM)] * 4,
        out_shape=[
            jax.ShapeDtypeStruct((size_x, size_y, size_z * WIDE), F32),
            jax.ShapeDtypeStruct((BASIS, WIDE), F32),
            jax.ShapeDtypeStruct((WIDE, WIDE), F32),
        ],
        scratch_shapes=[
            pltpu.VMEM((WIDE, 2 * WIDE), F32),
            pltpu.VMEM((WIDE, WIDE), F32),
            pltpu.VMEM((WIDE, WIDE), F32),
        ],
        compiler_params=pltpu.CompilerParams(vmem_limit_bytes=24 * 1024 * 1024),
    )(degree_shift, prior_parts, columns, total, other)
    return new_basis, projection, triangle


def solution(mesh):
    return jax.shard_map(
        cycle,
        mesh=mesh,
        in_specs=(P("gx", "gy", "gz"), P(None, "gx", "gy", "gz"), P()),
        out_specs=(P("gx", "gy", "gz"), P(), P()),
        check_vma=False,
    )
```
